512 devices in a mesh: row: 16 (over x_hi, z), col: 32 (over y, x_lo, core).
Axes of the slice: x: 4 (x_hi: 2, x_lo: 2; x = x_hi * 2 + x_lo), y: 8, z: 8, core: 2. Of those that a mesh axis runs over, the one named last changes fastest.
Arguments:
- h_blocks: bfloat16 [16, 32, 8, 128, 128], P('row', 'col'), as said below
- h_index: int32 [16, 32, 2, 8], P('row', 'col'), may hold values from 0 to 3, as said below
- z_blocks: bfloat16 [16, 32, 8, 128, 128], P('row', 'col'), as said below
- z_index: int32 [16, 32, 2, 8], P('row', 'col'), may hold values from 0 to 3, as said below
- keep_index: int32 [16, 32, 2, 8], P('row', 'col'), may hold values from 0 to 3, as said below
Outputs:
- filtered: float32 [16, 32, 4, 128, 128], P('row', 'col')
The draws below stay inside these ranges and needn't reach their ends.
Inputs may be any that keep to these rules, and one draw needn't show every extreme that they name: `h_blocks`: grid positions whose lists name the same H tile hold equal blocks. `z_blocks`: grid positions whose lists name the same Z tile hold equal blocks. `h_index`: each list holds 8 distinct block positions; grid positions that name the same H tile hold equal lists. `z_index`: each list holds 8 distinct block positions; grid positions that name the same Z tile hold equal lists. `keep_index`: each list holds 8 distinct block positions; the 2 grid positions with equal i and c hold equal lists.
All inputs are finite; a program needn't handle non-finite values.
Results may differ from the reference program's by a relative error of at most 0.0003.
Values may be sent and summed in bfloat16 or wider, within the bound.
No kernel may reach another device: no remote copies, remote signals or barrier semaphores. Data moves between devices by JAX's collectives and lax.ppermute only.
A program may use at most 64 MiB of HBM per device.

```python
import jax
import jax.numpy as jnp
from jax import lax

BLOCK = 128
TILE = 4
NNZ = 8
KEEP = 8
GRID = 16
LAYERS = 2
STEPS = 8


def grid_tiles():
    grid_row = jnp.arange(GRID, dtype=jnp.int32)[:, None] + jnp.zeros((1, GRID * LAYERS), jnp.int32)
    grid_col = jnp.arange(GRID * LAYERS, dtype=jnp.int32)[None, :] + jnp.zeros((GRID, 1), jnp.int32)
    column_slot = grid_col // LAYERS
    layer_slot = grid_col % LAYERS
    inner = (grid_row + column_slot + layer_slot * STEPS) % GRID
    return (grid_row, column_slot, inner)


def tile_values(key, tile_ids, stream_tag, factor):
    base = jax.random.fold_in(key, stream_tag)

    def one_tile(tile_id):
        sub_key = jax.random.fold_in(base, tile_id)
        values = jax.random.normal(sub_key, (NNZ, BLOCK, BLOCK), jnp.float32)
        return values * factor
    flat_ids = tile_ids.reshape(-1)
    values = jax.vmap(one_tile)(flat_ids)
    return values.reshape(tile_ids.shape + (NNZ, BLOCK, BLOCK))


def tile_positions(key, tile_ids, stream_tag, count, band):
    base = jax.random.fold_in(key, stream_tag)

    def one_tile(tile_id):
        shuffled = jax.random.permutation(jax.random.fold_in(base, tile_id), TILE * band)[:count]
        block_row = shuffled // band
        offset = shuffled % band - (band - 1) // 2
        block_col = (block_row + offset + TILE) % TILE
        return jnp.stack([block_row, block_col]).astype(jnp.int32)
    flat_ids = tile_ids.reshape(-1)
    places = jax.vmap(one_tile)(flat_ids)
    return places.reshape(tile_ids.shape + (2, count))


def h_tile_ids():
    grid_row, column_slot, inner = grid_tiles()
    return grid_row * GRID + inner


def z_tile_ids():
    grid_row, column_slot, inner = grid_tiles()
    return inner * GRID + column_slot


def draw_h_blocks(key, part):
    return tile_values(key, h_tile_ids(), 11, BLOCK ** (-0.5)).astype(jnp.bfloat16)


def draw_z_blocks(key, part):
    return tile_values(key, z_tile_ids(), 13, 1.0).astype(jnp.bfloat16)


def draw_h_index(key, part):
    return tile_positions(key, h_tile_ids(), 17, NNZ, min(3, TILE))


def draw_z_index(key, part):
    return tile_positions(key, z_tile_ids(), 19, NNZ, min(3, TILE))


def draw_keep_index(key, part):
    grid_row, column_slot, inner = grid_tiles()
    return tile_positions(key, grid_row * GRID + column_slot, 23, KEEP, min(5, TILE))


def setup_inputs(seed: int = 0) -> dict:
    key_of = jax.random.split(jax.random.key(seed), 6)
    h_blocks = draw_h_blocks(jax.random.fold_in(key_of[5], 71), 0)
    h_index = draw_h_index(jax.random.fold_in(key_of[5], 71), 0)
    z_blocks = draw_z_blocks(jax.random.fold_in(key_of[5], 71), 0)
    z_index = draw_z_index(jax.random.fold_in(key_of[5], 71), 0)
    keep_index = draw_keep_index(jax.random.fold_in(key_of[5], 71), 0)
    return dict(h_blocks=h_blocks, h_index=h_index, z_blocks=z_blocks, z_index=z_index, keep_index=keep_index)


def densify(blocks, places):
    count = blocks.shape[0]
    width = blocks.shape[1]
    slots = places[0] * TILE + places[1]
    selector = (jnp.arange(TILE * TILE, dtype=jnp.int32)[:, None] == slots[None, :]).astype(blocks.dtype)
    flat = jnp.dot(selector, blocks.reshape(count, width * width), preferred_element_type=jnp.float32)
    flat = flat.astype(blocks.dtype)
    return flat.reshape(TILE, TILE, width, width).transpose(0, 2, 1, 3).reshape(TILE * width, TILE * width)


def pick_blocks(dense, kept_pos):
    width = dense.shape[0] // TILE
    tiles = dense.reshape(TILE, width, TILE, width).transpose(0, 2, 1, 3).reshape(TILE * TILE, width * width)
    slots = kept_pos[0] * TILE + kept_pos[1]
    selector = (slots[:, None] == jnp.arange(TILE * TILE, dtype=jnp.int32)[None, :]).astype(jnp.float32)
    picked = jnp.dot(selector, tiles, precision=lax.Precision.HIGHEST, preferred_element_type=jnp.float32)
    return picked.reshape(kept_pos.shape[1], width, width)


def reference(h_blocks, h_index, z_blocks, z_index, keep_index):
    h_first = h_blocks[:, ::LAYERS]
    h_place = h_index[:, ::LAYERS]
    z_first = z_blocks[:, ::LAYERS]
    z_place = z_index[:, ::LAYERS]
    kept_all = keep_index[:, ::LAYERS]

    def one_tile(tile_flat):
        tile_row = tile_flat // GRID
        tile_col = tile_flat % GRID
        kept_pos = kept_all[tile_row, tile_col]

        def advance(running, offset):
            h_slot = (tile_col + offset) % GRID
            z_slot = (tile_row + offset) % GRID
            h_dense = densify(h_first[tile_row, h_slot], h_place[tile_row, h_slot])
            z_dense = densify(z_first[z_slot, tile_col], z_place[z_slot, tile_col])
            return running + jnp.dot(h_dense, z_dense, preferred_element_type=jnp.float32), None

        start = jnp.zeros((TILE * BLOCK, TILE * BLOCK), jnp.float32)
        running, unused = lax.scan(advance, start, jnp.arange(GRID, dtype=jnp.int32))
        return pick_blocks(running, kept_pos)

    result = lax.map(one_tile, jnp.arange(GRID * GRID, dtype=jnp.int32))
    result = result.reshape(GRID, GRID, LAYERS, KEEP // LAYERS, BLOCK, BLOCK)
    return result.reshape(GRID, GRID * LAYERS, KEEP // LAYERS, BLOCK, BLOCK)
```

```python
import functools

import jax
import jax.numpy as jnp
from jax import lax
from jax.experimental import pallas as pl
from jax.experimental.pallas import tpu as pltpu
from jax.sharding import PartitionSpec as P

TILE = 4
NNZ = 8
WIDTH = 128
GRID = 16
HALF = 8
SPAN = TILE * WIDTH
ROWS = NNZ * WIDTH + 16
BOTH = ("row", "col")


def even_pair(n):
    return n ^ 1


def odd_pair(n):
    return ((n - 1) ^ 1) + 1


def flat_id(i, c, role):
    layer = role ^ int((i + c) % GRID >= HALF)
    return i * 2 * GRID + c * 2 + layer


def route(step):
    pairs = []
    for i in range(GRID):
        for c in range(GRID):
            for role in range(2):
                z, y, x = step(i % HALF, c // 2, c % 2, role)
                pairs.append((flat_id(i, c, role), flat_id(i // HALF * HALF + z % HALF, (y % HALF) * 2 + x, role)))
    return pairs


def pair_of(kind, n, role):
    return even_pair(n) if kind == role else odd_pair(n)


def exchange_z(x, kind):
    return lax.ppermute(x, BOTH, route(lambda z, y, xl, r: (pair_of(kind, z, r), y, xl)))


def exchange_y(x, kind):
    return lax.ppermute(x, BOTH, route(lambda z, y, xl, r: (z, pair_of(kind, y, r), xl)))


def exchange_x(x):
    return lax.ppermute(x, BOTH, route(lambda z, y, xl, r: (z, y, xl ^ 1)))


def with_slots(blocks, places):
    slots = (places[0] * TILE + places[1]).astype(blocks.dtype)
    tail = jnp.pad(slots[None, :], ((0, ROWS - NNZ * WIDTH - 1), (0, WIDTH - NNZ)))
    return jnp.concatenate([blocks.reshape(NNZ * WIDTH, WIDTH), tail], axis=0)


def product_kernel(
    keep, hp, h1, h2, h3, zp, z1, z2, z3, z4, own, other, hd, zd, acc, idx_v, idx_s, sem
):
    i = lax.axis_index("row")
    j = lax.axis_index("col")
    c = j >> 1
    layer = j & 1
    z = i & 7
    y = c >> 1
    xl = c & 1
    role = layer ^ (((i + c) & 15) >> 3)

    def near(n, kind):
        even = n ^ 1
        odd = ((n - 1) ^ 1) + 1
        return jnp.where(role == kind, even, odd) & 7

    def h_at(yy, xx):
        return (z + 2 * yy + xx) & 7

    def z_at(zz):
        return (zz + c) & 7

    ya = near(y, 0)
    yb = near(y, 1)
    yab = near(yb, 0)
    p = near(z, 0)
    w = near(z, 1)
    pw = near(w, 0)
    wp = near(p, 1)
    pwp = near(wp, 0)
    wpw = near(pw, 1)
    pwpw = near(wpw, 0)
    tiles = [
        (hp, 0, h_at(y, xl)),
        (h1, 0, h_at(y, xl ^ 1)),
        (h2, 0, h_at(ya, xl)),
        (h2, 1, h_at(ya, xl ^ 1)),
        (h3, 0, h_at(yb, xl)),
        (h3, 1, h_at(yb, xl ^ 1)),
        (h3, 2, h_at(yab, xl)),
        (h3, 3, h_at(yab, xl ^ 1)),
        (zp, 0, z_at(z)),
        (z1, 0, z_at(p)),
        (z2, 0, z_at(w)),
        (z2, 1, z_at(pw)),
        (z3, 0, z_at(wp)),
        (z3, 1, z_at(pwp)),
        (z4, 0, z_at(wpw)),
        (z4, 1, z_at(pwpw)),
    ]
    for n, (buf, part, _) in enumerate(tiles):
        base = part * ROWS + NNZ * WIDTH
        idx_v[n : n + 1, :] = buf[base : base + 16, :].astype(jnp.float32).astype(jnp.int32)[0:1]
    copy = pltpu.make_async_copy(idx_v, idx_s, sem)
    copy.start()

    @pl.loop(0, HALF)
    def _(u):
        at = pl.multiple_of(u * SPAN, SPAN)
        hd[:, pl.ds(at, SPAN)] = jnp.zeros((SPAN, SPAN), hd.dtype)
        zd[pl.ds(at, SPAN), :] = jnp.zeros((SPAN, SPAN), zd.dtype)

    copy.wait()
    for n, (buf, part, u) in enumerate(tiles):
        for k in range(NNZ):
            slot = idx_s[n, k]
            block = buf[part * ROWS + k * WIDTH : part * ROWS + (k + 1) * WIDTH, :]
            r = (slot >> 2) * WIDTH
            q = (slot & 3) * WIDTH
            if n < HALF:
                hd[pl.ds(pl.multiple_of(r, WIDTH), WIDTH), pl.ds(pl.multiple_of(u * SPAN + q, WIDTH), WIDTH)] = block
            else:
                zd[pl.ds(pl.multiple_of(u * SPAN + r, WIDTH), WIDTH), pl.ds(pl.multiple_of(q, WIDTH), WIDTH)] = block
    for m in range(0, SPAN, 256):
        acc[m : m + 256, :] = jnp.dot(hd[m : m + 256, :], zd[...], preferred_element_type=jnp.float32)
    for q in range(TILE):
        for dst, first in ((own, layer * TILE), (other, (1 - layer) * TILE)):
            r = pl.multiple_of(keep[0, first + q] * WIDTH, WIDTH)
            s = pl.multiple_of(keep[1, first + q] * WIDTH, WIDTH)
            dst[q] = acc[pl.ds(r, WIDTH), pl.ds(s, WIDTH)]


def product(keep, *tiles):
    vmem = pl.BlockSpec(memory_space=pltpu.VMEM)
    half = jax.ShapeDtypeStruct((TILE, WIDTH, WIDTH), jnp.float32)
    return pl.pallas_call(
        product_kernel,
        out_shape=(half, half),
        in_specs=[pl.BlockSpec(memory_space=pltpu.SMEM)] + [vmem] * len(tiles),
        out_specs=(vmem, vmem),
        scratch_shapes=[
            pltpu.VMEM((SPAN, HALF * SPAN), jnp.bfloat16),
            pltpu.VMEM((HALF * SPAN, SPAN), jnp.bfloat16),
            pltpu.VMEM((SPAN, SPAN), jnp.float32),
            pltpu.VMEM((GRID, WIDTH), jnp.int32),
            pltpu.SMEM((GRID, WIDTH), jnp.int32),
            pltpu.SemaphoreType.DMA,
        ],
        compiler_params=pltpu.CompilerParams(vmem_limit_bytes=32 * 1024 * 1024),
        cost_estimate=pl.CostEstimate(
            flops=2 * SPAN * SPAN * SPAN * HALF, bytes_accessed=5 * 1024 * 1024, transcendentals=0
        ),
        name="product",
    )(keep, *tiles)


def per_device(h_blocks, h_index, z_blocks, z_index, keep_index):
    zp = with_slots(z_blocks[0, 0], z_index[0, 0])
    z1 = exchange_z(zp, 0)
    hp = with_slots(h_blocks[0, 0], h_index[0, 0])
    h1 = exchange_x(hp)
    z2 = exchange_z(jnp.concatenate([zp, z1], axis=0), 1)
    h2 = exchange_y(jnp.concatenate([hp, h1], axis=0), 0)
    z3 = exchange_z(z2, 0)
    h3 = exchange_y(jnp.concatenate([hp, h1, h2], axis=0), 1)
    z4 = exchange_z(z3, 1)
    own, other = product(keep_index[0, 0], hp, h1, h2, h3, zp, z1, z2, z3, z4)
    partner = lax.ppermute(other, "col", [(j, j ^ 1) for j in range(2 * GRID)])
    return (own + partner)[None, None]


def solution(mesh):
    return jax.shard_map(
        per_device,
        mesh=mesh,
        in_specs=(
            P("row", "col", None, None, None),
            P("row", "col", None, None),
            P("row", "col", None, None, None),
            P("row", "col", None, None),
            P("row", "col", None, None),
        ),
        out_specs=P("row", "col", None, None, None),
        check_vma=False,
    )
```

```python
import functools

import jax
import jax.numpy as jnp
from jax import lax
from jax.experimental import pallas as pl
from jax.experimental.pallas import tpu as pltpu
from jax.sharding import PartitionSpec as P

TILE = 4
NNZ = 8
WIDTH = 128
GRID = 16
HALF = 8
SPAN = TILE * WIDTH
ROWS = NNZ * WIDTH + 16
BOTH = ("row", "col")


def even_pair(n):
    return n ^ 1


def odd_pair(n):
    return ((n - 1) ^ 1) + 1


def flat_id(i, c, role):
    layer = role ^ int((i + c) % GRID >= HALF)
    return i * 2 * GRID + c * 2 + layer


def route(step):
    pairs = []
    for i in range(GRID):
        for c in range(GRID):
            for role in range(2):
                z, y, x = step(i % HALF, c // 2, c % 2, role)
                pairs.append((flat_id(i, c, role), flat_id(i // HALF * HALF + z % HALF, (y % HALF) * 2 + x, role)))
    return pairs


def pair_of(kind, n, role):
    return even_pair(n) if kind == role else odd_pair(n)


def exchange_z(x, kind):
    return lax.ppermute(x, BOTH, route(lambda z, y, xl, r: (pair_of(kind, z, r), y, xl)))


def exchange_y(x, kind):
    return lax.ppermute(x, BOTH, route(lambda z, y, xl, r: (z, pair_of(kind, y, r), xl)))


def exchange_x(x):
    return lax.ppermute(x, BOTH, route(lambda z, y, xl, r: (z, y, xl ^ 1)))


def pack_kernel(places_z, places_h, blocks_z, blocks_h, out_z, out_h, tail, sem):
    lane = lax.broadcasted_iota(jnp.int32, tail.shape[1:], 1)
    copies = []
    for n, (blocks, out) in enumerate(((blocks_z, out_z), (blocks_h, out_h))):
        copies.append(pltpu.make_async_copy(blocks, out.at[pl.ds(0, NNZ * WIDTH)], sem.at[n]))
        copies[-1].start()
    for n, (places, out) in enumerate(((places_z, out_z), (places_h, out_h))):
        slots = jnp.zeros(lane.shape, jnp.int32)
        for k in range(NNZ):
            slots = jnp.where(lane == k, places[0, k] * TILE + places[1, k], slots)
        tail[n] = slots.astype(jnp.float32).astype(tail.dtype)
        copies.append(
            pltpu.make_async_copy(
                tail.at[n], out.at[pl.ds(NNZ * WIDTH, ROWS - NNZ * WIDTH)], sem.at[2 + n]
            )
        )
        copies[-1].start()
    for copy in copies:
        copy.wait()


def pack(places_z, places_h, blocks_z, blocks_h):
    smem = pl.BlockSpec(memory_space=pltpu.SMEM)
    hbm = pl.BlockSpec(memory_space=pl.ANY)
    return pl.pallas_call(
        pack_kernel,
        out_shape=(jax.ShapeDtypeStruct((ROWS, WIDTH), blocks_z.dtype),) * 2,
        in_specs=[smem, smem, hbm, hbm],
        out_specs=(hbm, hbm),
        scratch_shapes=[
            pltpu.VMEM((2, ROWS - NNZ * WIDTH, WIDTH), blocks_z.dtype),
            pltpu.SemaphoreType.DMA((4,)),
        ],
        cost_estimate=pl.CostEstimate(flops=0, bytes_accessed=ROWS * WIDTH * 8, transcendentals=0),
        name="pack",
    )(places_z, places_h, blocks_z.reshape(NNZ * WIDTH, WIDTH), blocks_h.reshape(NNZ * WIDTH, WIDTH))


def near(n, kind, role):
    even = n ^ 1
    odd = ((n - 1) ^ 1) + 1
    return jnp.where(role == kind, even, odd) & 7


def position():
    i = lax.axis_index("row")
    j = lax.axis_index("col")
    c = j >> 1
    layer = j & 1
    role = layer ^ (((i + c) & 15) >> 3)
    return i & 7, c >> 1, c & 1, layer, role


def arrival_order():
    z, y, xl, _, role = position()
    ya = near(y, 0, role)
    yb = near(y, 1, role)
    yab = near(yb, 0, role)
    up = near(z, 0, role) - z

    def place(yy, xx):
        ahead = (2 * yy + xx - 2 * y - xl) & 7
        ahead = jnp.where((up & 7) == 1, ahead, -ahead) & 7
        return (0x23675410 >> (4 * ahead)) & 7

    return [place(yy, xx) for yy in (y, ya, yb, yab) for xx in (xl, xl ^ 1)]


def read_slots(parts, idx_v, idx_s, sem):
    for n, (buf, part) in enumerate(parts):
        base = part * ROWS + NNZ * WIDTH
        idx_v[n : n + 1, :] = buf[base : base + 16, :].astype(jnp.float32).astype(jnp.int32)[0:1]
    copy = pltpu.make_async_copy(idx_v, idx_s, sem)
    copy.start()
    return copy


def place_h(dense, late, buf, part, slots, n, turn):
    for k in range(NNZ):
        r = pl.ds(pl.multiple_of((slots[n, k] >> 2) * WIDTH, WIDTH), WIDTH)
        q = (slots[n, k] & 3) * WIDTH
        at = part * ROWS + k * WIDTH

        @pl.when(turn < EARLY)
        def _():
            dense[r, pl.ds(pl.multiple_of(turn * SPAN + q, WIDTH), WIDTH)] = buf[at : at + WIDTH, :]

        @pl.when(turn >= EARLY)
        def _():
            late[r, pl.ds(pl.multiple_of((turn - EARLY) * SPAN + q, WIDTH), WIDTH)] = buf[at : at + WIDTH, :]


def place_z(dense, buf, part, slots, n, turn):
    for k in range(NNZ):
        r = turn * SPAN + (slots[n, k] >> 2) * WIDTH
        q = (slots[n, k] & 3) * WIDTH
        at = part * ROWS + k * WIDTH
        dense[pl.ds(pl.multiple_of(r, WIDTH), WIDTH), pl.ds(pl.multiple_of(q, WIDTH), WIDTH)] = buf[at : at + WIDTH, :]


EARLY = 6
LATE = HALF - EARLY


def early_kernel(hp, h1, h2, h3, h4, zp, z1, z2, z3, acc, late, hd, zd, idx_v, idx_s, sem):
    h_parts = [(hp, 0), (h1, 0), (h2, 0), (h2, 1), (h3, 0), (h3, 1), (h4, 0), (h4, 1)]
    z_parts = [(zp, 0), (z1, 0), (z2, 0), (z2, 1), (z3, 0), (z3, 1)]
    copy = read_slots(h_parts + z_parts, idx_v, idx_s, sem)

    late[...] = jnp.zeros_like(late)

    @pl.loop(0, EARLY)
    def _(u):
        at = pl.multiple_of(u * SPAN, SPAN)
        hd[:, pl.ds(at, SPAN)] = jnp.zeros((SPAN, SPAN), hd.dtype)
        zd[pl.ds(at, SPAN), :] = jnp.zeros((SPAN, SPAN), zd.dtype)

    turns = arrival_order()
    copy.wait()
    for n, (buf, part) in enumerate(h_parts):
        place_h(hd, late, buf, part, idx_s, n, turns[n])
    for n, (buf, part) in enumerate(z_parts):
        place_z(zd, buf, part, idx_s, HALF + n, n)
    for m in range(0, SPAN, 256):
        acc[m : m + 256, :] = jnp.dot(
            hd[m : m + 256, :], zd[...], preferred_element_type=jnp.float32
        )


def late_kernel(keep, hd, acc, z4, own, other, zd, total, idx_v, idx_s, sem):
    parts = [(z4, 0), (z4, 1)]
    copy = read_slots(parts, idx_v, idx_s, sem)
    zd[...] = jnp.zeros_like(zd)
    layer = lax.axis_index("col") & 1
    copy.wait()
    for n, (buf, part) in enumerate(parts):
        place_z(zd, buf, part, idx_s, n, n)
    for m in range(0, SPAN, 256):
        total[m : m + 256, :] = acc[m : m + 256, :] + jnp.dot(
            hd[m : m + 256, :], zd[...], preferred_element_type=jnp.float32
        )
    for q in range(TILE):
        for dst, first in ((own, layer * TILE), (other, (1 - layer) * TILE)):
            r = pl.multiple_of(keep[0, first + q] * WIDTH, WIDTH)
            s = pl.multiple_of(keep[1, first + q] * WIDTH, WIDTH)
            dst[q] = total[pl.ds(r, WIDTH), pl.ds(s, WIDTH)]


def slot_scratch(rows):
    return [
        pltpu.VMEM((rows, WIDTH), jnp.int32),
        pltpu.SMEM((rows, WIDTH), jnp.int32),
        pltpu.SemaphoreType.DMA,
    ]


def early_product(*tiles):
    vmem = pl.BlockSpec(memory_space=pltpu.VMEM)
    return pl.pallas_call(
        early_kernel,
        out_shape=(
            jax.ShapeDtypeStruct((SPAN, SPAN), jnp.float32),
            jax.ShapeDtypeStruct((SPAN, LATE * SPAN), jnp.bfloat16),
        ),
        in_specs=[vmem] * len(tiles),
        out_specs=(vmem, vmem),
        scratch_shapes=[
            pltpu.VMEM((SPAN, EARLY * SPAN), jnp.bfloat16),
            pltpu.VMEM((EARLY * SPAN, SPAN), jnp.bfloat16),
        ]
        + slot_scratch(GRID),
        compiler_params=pltpu.CompilerParams(vmem_limit_bytes=12 * 1024 * 1024),
        cost_estimate=pl.CostEstimate(
            flops=2 * SPAN * SPAN * SPAN * EARLY, bytes_accessed=5 * 1024 * 1024, transcendentals=0
        ),
        name="early",
    )(*tiles)


def late_product(keep, hd, acc, z4):
    vmem = pl.BlockSpec(memory_space=pltpu.VMEM)
    half = jax.ShapeDtypeStruct((TILE, WIDTH, WIDTH), jnp.float32)
    return pl.pallas_call(
        late_kernel,
        out_shape=(half, half),
        in_specs=[pl.BlockSpec(memory_space=pltpu.SMEM), vmem, vmem, vmem],
        out_specs=(vmem, vmem),
        scratch_shapes=[
            pltpu.VMEM((LATE * SPAN, SPAN), jnp.bfloat16),
            pltpu.VMEM((SPAN, SPAN), jnp.float32),
        ]
        + slot_scratch(8),
        compiler_params=pltpu.CompilerParams(vmem_limit_bytes=4 * 1024 * 1024),
        cost_estimate=pl.CostEstimate(
            flops=2 * SPAN * SPAN * SPAN * LATE, bytes_accessed=2 * 1024 * 1024, transcendentals=0
        ),
        name="late",
    )(keep, hd, acc, z4)


def per_device(h_blocks, h_index, z_blocks, z_index, keep_index):
    zp, hp = pack(z_index[0, 0], h_index[0, 0], z_blocks[0, 0], h_blocks[0, 0])
    z1 = exchange_z(zp, 0)
    h1 = exchange_x(hp)
    z2 = exchange_z(jnp.concatenate([zp, z1], axis=0), 1)
    h01 = jnp.concatenate([hp, h1], axis=0)
    h2 = exchange_y(h01, 0)
    h3 = exchange_y(h01, 1)
    z3 = exchange_z(z2, 0)
    h4 = exchange_y(h2, 1)
    z4 = exchange_z(z3, 1)
    acc, hd = early_product(hp, h1, h2, h3, h4, zp, z1, z2, z3)
    own, other = late_product(keep_index[0, 0], hd, acc, z4)
    both = lax.all_gather(
        other, "col", axis_index_groups=[[2 * c, 2 * c + 1] for c in range(GRID)], tiled=False
    )
    partner = lax.dynamic_index_in_dim(both, 1 - (lax.axis_index("col") & 1), 0, keepdims=False)
    return (own + partner)[None, None]


def solution(mesh):
    return jax.shard_map(
        per_device,
        mesh=mesh,
        in_specs=(
            P("row", "col", None, None, None),
            P("row", "col", None, None),
            P("row", "col", None, None, None),
            P("row", "col", None, None),
            P("row", "col", None, None),
        ),
        out_specs=P("row", "col", None, None, None),
        check_vma=False,
    )
```

```python
import functools

import jax
import jax.numpy as jnp
from jax import lax
from jax.experimental import pallas as pl
from jax.experimental.pallas import tpu as pltpu
from jax.sharding import PartitionSpec as P

TILE = 4
NNZ = 8
WIDTH = 128
GRID = 16
HALF = 8
SPAN = TILE * WIDTH
ROWS = NNZ * WIDTH + 16
BOTH = ("row", "col")


def even_pair(n):
    return n ^ 1


def odd_pair(n):
    return ((n - 1) ^ 1) + 1


def flat_id(i, c, role):
    layer = role ^ int((i + c) % GRID >= HALF)
    return i * 2 * GRID + c * 2 + layer


def route(step):
    pairs = []
    for i in range(GRID):
        for c in range(GRID):
            for role in range(2):
                z, y, x = step(i % HALF, c // 2, c % 2, role)
                pairs.append((flat_id(i, c, role), flat_id(i // HALF * HALF + z % HALF, (y % HALF) * 2 + x, role)))
    return pairs


def pair_of(kind, n, role):
    return even_pair(n) if kind == role else odd_pair(n)


def exchange_z(x, kind):
    return lax.ppermute(x, BOTH, route(lambda z, y, xl, r: (pair_of(kind, z, r), y, xl)))


def exchange_y(x, kind):
    return lax.ppermute(x, BOTH, route(lambda z, y, xl, r: (z, pair_of(kind, y, r), xl)))


def exchange_x(x):
    return lax.ppermute(x, BOTH, route(lambda z, y, xl, r: (z, y, xl ^ 1)))


def pack_kernel(places_z, places_h, blocks_z, blocks_h, out_z, out_h, sem):
    lane = lax.broadcasted_iota(jnp.int32, (ROWS - NNZ * WIDTH, WIDTH), 1)
    copies = []
    for n, (blocks, out) in enumerate(((blocks_z, out_z), (blocks_h, out_h))):
        copies.append(pltpu.make_async_copy(blocks, out.at[pl.ds(0, NNZ * WIDTH)], sem.at[n]))
        copies[-1].start()
    for places, out in ((places_z, out_z), (places_h, out_h)):
        slots = jnp.zeros(lane.shape, jnp.int32)
        for k in range(NNZ):
            slots = jnp.where(lane == k, places[0, k] * TILE + places[1, k], slots)
        out[pl.ds(NNZ * WIDTH, ROWS - NNZ * WIDTH), :] = slots.astype(jnp.float32).astype(out.dtype)
    for copy in copies:
        copy.wait()


PACK_LIMIT = 56 * 1024 * 1024


def pack(places_z, places_h, blocks_z, blocks_h):
    smem = pl.BlockSpec(memory_space=pltpu.SMEM)
    hbm = pl.BlockSpec(memory_space=pl.ANY)
    vmem = pl.BlockSpec(memory_space=pltpu.VMEM)
    return pl.pallas_call(
        pack_kernel,
        out_shape=(jax.ShapeDtypeStruct((ROWS, WIDTH), blocks_z.dtype),) * 2,
        in_specs=[smem, smem, hbm, hbm],
        out_specs=(vmem, vmem),
        scratch_shapes=[pltpu.SemaphoreType.DMA((2,))],
        compiler_params=pltpu.CompilerParams(vmem_limit_bytes=PACK_LIMIT),
        cost_estimate=pl.CostEstimate(flops=0, bytes_accessed=ROWS * WIDTH * 8, transcendentals=0),
        name="pack",
    )(places_z, places_h, blocks_z.reshape(NNZ * WIDTH, WIDTH), blocks_h.reshape(NNZ * WIDTH, WIDTH))


def near(n, kind, role):
    even = n ^ 1
    odd = ((n - 1) ^ 1) + 1
    return jnp.where(role == kind, even, odd) & 7


def position():
    i = lax.axis_index("row")
    j = lax.axis_index("col")
    c = j >> 1
    layer = j & 1
    role = layer ^ (((i + c) & 15) >> 3)
    return i & 7, c >> 1, c & 1, layer, role


def offsets():
    z, y, xl, _, role = position()
    ya = near(y, 0, role)
    yb = near(y, 1, role)
    yab = near(yb, 0, role)
    up = near(z, 0, role) - z
    of_h = [(2 * (yy - y) + xx - xl) & 7 for yy in (y, ya, yb, yab) for xx in (xl, xl ^ 1)]
    of_z = [(up * n) & 7 for n in (0, 1, -1, -2, 2, 3, -3, 4)]
    return of_h, of_z


def read_slots(parts, idx_v, idx_s, sem):
    for n, (buf, part) in enumerate(parts):
        base = part * ROWS + NNZ * WIDTH
        idx_v[n : n + 1, :] = buf[base : base + 16, :].astype(jnp.float32).astype(jnp.int32)[0:1]
    copy = pltpu.make_async_copy(idx_v, idx_s, sem)
    copy.start()
    return copy


def place(buf, part, slots, n, put):
    for k in range(NNZ):
        row = pl.multiple_of((slots[n, k] >> 2) * WIDTH, WIDTH)
        col = pl.multiple_of((slots[n, k] & 3) * WIDTH, WIDTH)
        at = part * ROWS + k * WIDTH
        put(row, col, buf[at : at + WIDTH, :])


def into_h(dense, turn):
    def put(row, col, block):
        dense[pl.ds(row, WIDTH), pl.ds(pl.multiple_of(turn * SPAN + col, WIDTH), WIDTH)] = block

    return put


def into_z(dense, turn):
    def put(row, col, block):
        dense[pl.ds(pl.multiple_of(turn * SPAN + row, WIDTH), WIDTH), pl.ds(col, WIDTH)] = block

    return put


LATE = 3
EARLY = HALF - LATE


def early_turn(ahead):
    return jnp.where(ahead < 3, ahead, ahead - 3)


def early_kernel(hp, h1, h2, h3, zp, z1, z2, z3, acc, late_h, late_z, hd, zd, idx_v, idx_s, sem):
    h_parts = [(hp, 0), (h1, 0), (h2, 0), (h2, 1), (h3, 0), (h3, 1)]
    z_parts = [(zp, 0), (z1, 0), (z2, 0), (z2, 1), (z3, 0), (z3, 1)]
    copy = read_slots(h_parts + z_parts, idx_v, idx_s, sem)
    late_h[...] = jnp.zeros_like(late_h)
    late_z[...] = jnp.zeros_like(late_z)

    @pl.loop(0, EARLY)
    def _(u):
        at = pl.multiple_of(u * SPAN, SPAN)
        hd[:, pl.ds(at, SPAN)] = jnp.zeros((SPAN, SPAN), hd.dtype)
        zd[pl.ds(at, SPAN), :] = jnp.zeros((SPAN, SPAN), zd.dtype)

    of_h, of_z = offsets()
    copy.wait()
    for n, (buf, part) in enumerate(h_parts):
        ahead = of_h[n]
        if n in (3, 5):
            is_late = (ahead >= 3) & (ahead <= 5)

            @pl.when(is_late)
            def _():
                place(buf, part, idx_s, n, into_h(late_h, ahead - 3))

            @pl.when(jnp.logical_not(is_late))
            def _():
                place(buf, part, idx_s, n, into_h(hd, early_turn(ahead)))
        else:
            place(buf, part, idx_s, n, into_h(hd, early_turn(ahead)))
    for n, (buf, part) in enumerate(z_parts):
        if n == 5:
            put = into_z(late_z, of_z[n] - 3)
        else:
            put = into_z(zd, early_turn(of_z[n]))
        place(buf, part, idx_s, len(h_parts) + n, put)
    for m in range(0, SPAN, 256):
        acc[m : m + 256, :] = jnp.dot(hd[m : m + 256, :], zd[...], preferred_element_type=jnp.float32)


def middle_kernel(h4, late_h, out_h, idx_v, idx_s, sem):
    parts = [(h4, 0), (h4, 1)]
    copy = read_slots(parts, idx_v, idx_s, sem)
    of_h, _ = offsets()
    copy.wait()
    for n, (buf, part) in enumerate(parts):
        place(buf, part, idx_s, n, into_h(out_h, of_h[6 + n] - 3))


def late_kernel(keep, acc, hd, late_z, z4, own, other, zd, total, idx_v, idx_s, sem):
    parts = [(z4, 0), (z4, 1)]
    copy = read_slots(parts, idx_v, idx_s, sem)
    _, of_z = offsets()
    layer = lax.axis_index("col") & 1
    copy.wait()
    for n, (buf, part) in enumerate(parts):
        place(buf, part, idx_s, n, into_z(zd, of_z[6 + n] - 3))
    for m in range(0, SPAN, 256):
        total[m : m + 256, :] = acc[m : m + 256, :] + jnp.dot(
            hd[m : m + 256, :], zd[...], preferred_element_type=jnp.float32
        )
    for q in range(TILE):
        for dst, first in ((own, layer * TILE), (other, (1 - layer) * TILE)):
            r = pl.multiple_of(keep[0, first + q] * WIDTH, WIDTH)
            s = pl.multiple_of(keep[1, first + q] * WIDTH, WIDTH)
            dst[q] = total[pl.ds(r, WIDTH), pl.ds(s, WIDTH)]


def slot_scratch(rows):
    return [
        pltpu.VMEM((rows, WIDTH), jnp.int32),
        pltpu.SMEM((rows, WIDTH), jnp.int32),
        pltpu.SemaphoreType.DMA,
    ]


VMEM = pl.BlockSpec(memory_space=pltpu.VMEM)
MIDDLE_FLOPS = 2 * SPAN * SPAN * SPAN * 32
LATE_H = jax.ShapeDtypeStruct((SPAN, LATE * SPAN), jnp.bfloat16)
LATE_Z = jax.ShapeDtypeStruct((LATE * SPAN, SPAN), jnp.bfloat16)


def early_product(*tiles):
    return pl.pallas_call(
        early_kernel,
        out_shape=(jax.ShapeDtypeStruct((SPAN, SPAN), jnp.float32), LATE_H, LATE_Z),
        in_specs=[VMEM] * len(tiles),
        out_specs=(VMEM, VMEM, VMEM),
        scratch_shapes=[
            pltpu.VMEM((SPAN, EARLY * SPAN), jnp.bfloat16),
            pltpu.VMEM((EARLY * SPAN, SPAN), jnp.bfloat16),
        ]
        + slot_scratch(GRID),
        compiler_params=pltpu.CompilerParams(vmem_limit_bytes=14 * 1024 * 1024),
        cost_estimate=pl.CostEstimate(
            flops=2 * SPAN * SPAN * SPAN * EARLY, bytes_accessed=5 * 1024 * 1024, transcendentals=0
        ),
        name="early",
    )(*tiles)


def middle_product(h4, late_h):
    return pl.pallas_call(
        middle_kernel,
        out_shape=LATE_H,
        in_specs=[VMEM] * 2,
        out_specs=VMEM,
        input_output_aliases={1: 0},
        scratch_shapes=slot_scratch(8),
        compiler_params=pltpu.CompilerParams(vmem_limit_bytes=8 * 1024 * 1024),
        cost_estimate=pl.CostEstimate(flops=MIDDLE_FLOPS, bytes_accessed=1024 * 1024, transcendentals=0),
        name="middle",
    )(h4, late_h)


def late_product(keep, acc, late_h, late_z, z4):
    half = jax.ShapeDtypeStruct((TILE, WIDTH, WIDTH), jnp.float32)
    own, other, _ = pl.pallas_call(
        late_kernel,
        out_shape=(half, half, LATE_Z),
        in_specs=[pl.BlockSpec(memory_space=pltpu.SMEM)] + [VMEM] * 4,
        out_specs=(VMEM,) * 3,
        input_output_aliases={3: 2},
        scratch_shapes=[pltpu.VMEM((SPAN, SPAN), jnp.float32)] + slot_scratch(8),
        compiler_params=pltpu.CompilerParams(vmem_limit_bytes=10 * 1024 * 1024),
        cost_estimate=pl.CostEstimate(
            flops=2 * SPAN * SPAN * SPAN * LATE, bytes_accessed=2 * 1024 * 1024, transcendentals=0
        ),
        name="late",
    )(keep, acc, late_h, late_z, z4)
    return own, other


def per_device(h_blocks, h_index, z_blocks, z_index, keep_index):
    zp, hp = pack(z_index[0, 0], h_index[0, 0], z_blocks[0, 0], h_blocks[0, 0])
    z1 = exchange_z(zp, 0)
    h1 = exchange_x(hp)
    z2 = exchange_z(jnp.concatenate([zp, z1], axis=0), 1)
    h01 = jnp.concatenate([hp, h1], axis=0)
    h2 = exchange_y(h01, 0)
    h3 = exchange_y(h01, 1)
    z3 = exchange_z(z2, 0)
    h4 = exchange_y(h2, 1)
    z4 = exchange_z(z3, 1)
    acc, late_h, late_z = early_product(hp, h1, h2, h3, zp, z1, z2, z3)
    late_h = middle_product(h4, late_h)
    own, other = late_product(keep_index[0, 0], acc, late_h, late_z, z4)
    both = lax.all_gather(
        other, "col", axis_index_groups=[[2 * c, 2 * c + 1] for c in range(GRID)], tiled=False
    )
    partner = lax.dynamic_index_in_dim(both, 1 - (lax.axis_index("col") & 1), 0, keepdims=False)
    return (own + partner)[None, None]


def solution(mesh):
    return jax.shard_map(
        per_device,
        mesh=mesh,
        in_specs=(
            P("row", "col", None, None, None),
            P("row", "col", None, None),
            P("row", "col", None, None, None),
            P("row", "col", None, None),
            P("row", "col", None, None),
        ),
        out_specs=P("row", "col", None, None, None),
        check_vma=False,
    )
```

```python
import functools

import jax
import jax.numpy as jnp
from jax import lax
from jax.experimental import pallas as pl
from jax.experimental.pallas import tpu as pltpu
from jax.sharding import PartitionSpec as P

TILE = 4
NNZ = 8
WIDTH = 128
GRID = 16
HALF = 8
SPAN = TILE * WIDTH
ROWS = NNZ * WIDTH + 16
BOTH = ("row", "col")


def even_pair(n):
    return n ^ 1


def odd_pair(n):
    return ((n - 1) ^ 1) + 1


def flat_id(i, c, role):
    layer = role ^ int((i + c) % GRID >= HALF)
    return i * 2 * GRID + c * 2 + layer


def route(step):
    pairs = []
    for i in range(GRID):
        for c in range(GRID):
            for role in range(2):
                z, y, x = step(i % HALF, c // 2, c % 2, role)
                pairs.append((flat_id(i, c, role), flat_id(i // HALF * HALF + z % HALF, (y % HALF) * 2 + x, role)))
    return pairs


def pair_of(kind, n, role):
    return even_pair(n) if kind == role else odd_pair(n)


def exchange_z(x, kind):
    return lax.ppermute(x, BOTH, route(lambda z, y, xl, r: (pair_of(kind, z, r), y, xl)))


def exchange_y(x, kind):
    return lax.ppermute(x, BOTH, route(lambda z, y, xl, r: (z, pair_of(kind, y, r), xl)))


def exchange_x(x):
    return lax.ppermute(x, BOTH, route(lambda z, y, xl, r: (z, y, xl ^ 1)))


def pack_kernel(places_z, places_h, blocks_z, blocks_h, out_z, out_h, sem):
    lane = lax.broadcasted_iota(jnp.int32, (ROWS - NNZ * WIDTH, WIDTH), 1)
    copies = []
    for n, (blocks, out) in enumerate(((blocks_z, out_z), (blocks_h, out_h))):
        copies.append(pltpu.make_async_copy(blocks, out.at[pl.ds(0, NNZ * WIDTH)], sem.at[n]))
        copies[-1].start()
    for places, out in ((places_z, out_z), (places_h, out_h)):
        slots = jnp.zeros(lane.shape, jnp.int32)
        for k in range(NNZ):
            slots = jnp.where(lane == k, places[0, k] * TILE + places[1, k], slots)
        out[pl.ds(NNZ * WIDTH, ROWS - NNZ * WIDTH), :] = slots.astype(jnp.float32).astype(out.dtype)
    for copy in copies:
        copy.wait()


PACK_LIMIT = 56 * 1024 * 1024


def pack(places_z, places_h, blocks_z, blocks_h):
    smem = pl.BlockSpec(memory_space=pltpu.SMEM)
    hbm = pl.BlockSpec(memory_space=pl.ANY)
    vmem = pl.BlockSpec(memory_space=pltpu.VMEM)
    return pl.pallas_call(
        pack_kernel,
        out_shape=(pltpu.VMEM((ROWS, WIDTH), blocks_z.dtype),) * 2,
        in_specs=[smem, smem, hbm, hbm],
        out_specs=(vmem, vmem),
        scratch_shapes=[pltpu.SemaphoreType.DMA((2,))],
        compiler_params=pltpu.CompilerParams(vmem_limit_bytes=PACK_LIMIT),
        cost_estimate=pl.CostEstimate(flops=0, bytes_accessed=ROWS * WIDTH * 8, transcendentals=0),
        name="pack",
    )(places_z, places_h, blocks_z.reshape(NNZ * WIDTH, WIDTH), blocks_h.reshape(NNZ * WIDTH, WIDTH))


def join_kernel(a, b, out):
    out[: a.shape[0], :] = a[...]
    out[a.shape[0] :, :] = b[...]


def join(a, b):
    vmem = pl.BlockSpec(memory_space=pltpu.VMEM)
    rows = a.shape[0] + b.shape[0]
    return pl.pallas_call(
        join_kernel,
        out_shape=jax.ShapeDtypeStruct((rows, WIDTH), a.dtype),
        in_specs=[vmem, vmem],
        out_specs=vmem,
        compiler_params=pltpu.CompilerParams(vmem_limit_bytes=4 * 1024 * 1024),
        cost_estimate=pl.CostEstimate(flops=0, bytes_accessed=rows * WIDTH * 4, transcendentals=0),
        name="join",
    )(a, b)


def near(n, kind, role):
    even = n ^ 1
    odd = ((n - 1) ^ 1) + 1
    return jnp.where(role == kind, even, odd) & 7


def position():
    i = lax.axis_index("row")
    j = lax.axis_index("col")
    c = j >> 1
    layer = j & 1
    role = layer ^ (((i + c) & 15) >> 3)
    return i & 7, c >> 1, c & 1, layer, role


def offsets():
    z, y, xl, _, role = position()
    ya = near(y, 0, role)
    yb = near(y, 1, role)
    yab = near(yb, 0, role)
    up = near(z, 0, role) - z
    of_h = [(2 * (yy - y) + xx - xl) & 7 for yy in (y, ya, yb, yab) for xx in (xl, xl ^ 1)]
    of_z = [(up * n) & 7 for n in (0, 1, -1, -2, 2, 3, -3, 4)]
    return of_h, of_z


class Slots:
    def __init__(self, parts):
        self.rows = []
        for buf, part in parts:
            base = part * ROWS + NNZ * WIDTH
            self.rows.append(buf[base : base + 16, :].astype(jnp.float32).astype(jnp.int32))

    def __getitem__(self, at):
        n, k = at
        return self.rows[n][0, k]


def place(buf, part, slots, n, put):
    for k in range(NNZ):
        row = pl.multiple_of((slots[n, k] >> 2) * WIDTH, WIDTH)
        col = pl.multiple_of((slots[n, k] & 3) * WIDTH, WIDTH)
        at = part * ROWS + k * WIDTH
        put(row, col, buf[at : at + WIDTH, :])


def into_h(dense, turn):
    def put(row, col, block):
        dense[pl.ds(row, WIDTH), pl.ds(pl.multiple_of(turn * SPAN + col, WIDTH), WIDTH)] = block

    return put


def into_z(dense, turn):
    def put(row, col, block):
        dense[pl.ds(pl.multiple_of(turn * SPAN + row, WIDTH), WIDTH), pl.ds(col, WIDTH)] = block

    return put


LATE = 3
EARLY = HALF - LATE


def early_turn(ahead):
    return jnp.where(ahead < 3, ahead, ahead - 3)


def early_kernel(hp, h1, h2, h3, zp, z1, z2, z3, acc, late_h, late_z, hd, zd):
    h_parts = [(hp, 0), (h1, 0), (h2, 0), (h2, 1), (h3, 0), (h3, 1)]
    z_parts = [(zp, 0), (z1, 0), (z2, 0), (z2, 1), (z3, 0), (z3, 1)]
    slots = Slots(h_parts + z_parts)
    late_h[...] = jnp.zeros_like(late_h)
    late_z[...] = jnp.zeros_like(late_z)

    @pl.loop(0, EARLY)
    def _(u):
        at = pl.multiple_of(u * SPAN, SPAN)
        hd[:, pl.ds(at, SPAN)] = jnp.zeros((SPAN, SPAN), hd.dtype)
        zd[pl.ds(at, SPAN), :] = jnp.zeros((SPAN, SPAN), zd.dtype)

    of_h, of_z = offsets()
    for n, (buf, part) in enumerate(h_parts):
        ahead = of_h[n]
        if n in (3, 5):
            is_late = (ahead >= 3) & (ahead <= 5)

            @pl.when(is_late)
            def _():
                place(buf, part, slots, n, into_h(late_h, ahead - 3))

            @pl.when(jnp.logical_not(is_late))
            def _():
                place(buf, part, slots, n, into_h(hd, early_turn(ahead)))
        else:
            place(buf, part, slots, n, into_h(hd, early_turn(ahead)))
    for n, (buf, part) in enumerate(z_parts):
        if n == 5:
            put = into_z(late_z, of_z[n] - 3)
        else:
            put = into_z(zd, early_turn(of_z[n]))
        place(buf, part, slots, len(h_parts) + n, put)
    for m in range(0, SPAN, 256):
        acc[m : m + 256, :] = jnp.dot(hd[m : m + 256, :], zd[...], preferred_element_type=jnp.float32)


def middle_kernel(h4, late_h, out_h):
    parts = [(h4, 0), (h4, 1)]
    slots = Slots(parts)
    of_h, _ = offsets()
    for n, (buf, part) in enumerate(parts):
        place(buf, part, slots, n, into_h(out_h, of_h[6 + n] - 3))


def late_kernel(keep, acc, hd, late_z, z4, own, other, zd, total):
    parts = [(z4, 0), (z4, 1)]
    slots = Slots(parts)
    _, of_z = offsets()
    layer = lax.axis_index("col") & 1
    for n, (buf, part) in enumerate(parts):
        place(buf, part, slots, n, into_z(zd, of_z[6 + n] - 3))
    for m in range(0, SPAN, 256):
        total[m : m + 256, :] = acc[m : m + 256, :] + jnp.dot(
            hd[m : m + 256, :], zd[...], preferred_element_type=jnp.float32
        )
    for q in range(TILE):
        for dst, first in ((own, layer * TILE), (other, (1 - layer) * TILE)):
            r = pl.multiple_of(keep[0, first + q] * WIDTH, WIDTH)
            s = pl.multiple_of(keep[1, first + q] * WIDTH, WIDTH)
            dst[q] = total[pl.ds(r, WIDTH), pl.ds(s, WIDTH)]


VMEM = pl.BlockSpec(memory_space=pltpu.VMEM)
MIDDLE_FLOPS = 2 * SPAN * SPAN * SPAN * 32
LATE_H = jax.ShapeDtypeStruct((SPAN, LATE * SPAN), jnp.bfloat16)
LATE_Z = jax.ShapeDtypeStruct((LATE * SPAN, SPAN), jnp.bfloat16)


def early_product(*tiles):
    return pl.pallas_call(
        early_kernel,
        out_shape=(jax.ShapeDtypeStruct((SPAN, SPAN), jnp.float32), LATE_H, LATE_Z),
        in_specs=[VMEM] * len(tiles),
        out_specs=(VMEM, VMEM, VMEM),
        scratch_shapes=[
            pltpu.VMEM((SPAN, EARLY * SPAN), jnp.bfloat16),
            pltpu.VMEM((EARLY * SPAN, SPAN), jnp.bfloat16),
        ],
        compiler_params=pltpu.CompilerParams(vmem_limit_bytes=14 * 1024 * 1024),
        cost_estimate=pl.CostEstimate(
            flops=2 * SPAN * SPAN * SPAN * EARLY, bytes_accessed=5 * 1024 * 1024, transcendentals=0
        ),
        name="early",
    )(*tiles)


def middle_product(h4, late_h):
    return pl.pallas_call(
        middle_kernel,
        out_shape=LATE_H,
        in_specs=[VMEM] * 2,
        out_specs=VMEM,
        input_output_aliases={1: 0},
        compiler_params=pltpu.CompilerParams(vmem_limit_bytes=8 * 1024 * 1024),
        cost_estimate=pl.CostEstimate(flops=MIDDLE_FLOPS, bytes_accessed=1024 * 1024, transcendentals=0),
        name="middle",
    )(h4, late_h)


def late_product(keep, acc, late_h, late_z, z4):
    half = jax.ShapeDtypeStruct((TILE, WIDTH, WIDTH), jnp.float32)
    own, other, _ = pl.pallas_call(
        late_kernel,
        out_shape=(half, half, LATE_Z),
        in_specs=[pl.BlockSpec(memory_space=pltpu.SMEM)] + [VMEM] * 4,
        out_specs=(VMEM,) * 3,
        input_output_aliases={3: 2},
        scratch_shapes=[pltpu.VMEM((SPAN, SPAN), jnp.float32)],
        compiler_params=pltpu.CompilerParams(vmem_limit_bytes=10 * 1024 * 1024),
        cost_estimate=pl.CostEstimate(
            flops=2 * SPAN * SPAN * SPAN * LATE, bytes_accessed=2 * 1024 * 1024, transcendentals=0
        ),
        name="late",
    )(keep, acc, late_h, late_z, z4)
    return own, other


def per_device(h_blocks, h_index, z_blocks, z_index, keep_index):
    zp, hp = pack(z_index[0, 0], h_index[0, 0], z_blocks[0, 0], h_blocks[0, 0])
    z1 = exchange_z(zp, 0)
    h1 = exchange_x(hp)
    z2 = exchange_z(join(zp, z1), 1)
    h01 = join(hp, h1)
    h2 = exchange_y(h01, 0)
    h3 = exchange_y(h01, 1)
    z3 = exchange_z(z2, 0)
    h4 = exchange_y(h2, 1)
    z4 = exchange_z(z3, 1)
    acc, late_h, late_z = early_product(hp, h1, h2, h3, zp, z1, z2, z3)
    late_h = middle_product(h4, late_h)
    own, other = late_product(keep_index[0, 0], acc, late_h, late_z, z4)
    both = lax.all_gather(
        other, "col", axis_index_groups=[[2 * c, 2 * c + 1] for c in range(GRID)], tiled=False
    )
    partner = lax.dynamic_index_in_dim(both, 1 - (lax.axis_index("col") & 1), 0, keepdims=False)
    return (own + partner)[None, None]


def solution(mesh):
    return jax.shard_map(
        per_device,
        mesh=mesh,
        in_specs=(
            P("row", "col", None, None, None),
            P("row", "col", None, None),
            P("row", "col", None, None, None),
            P("row", "col", None, None),
            P("row", "col", None, None),
        ),
        out_specs=P("row", "col", None, None, None),
        check_vma=False,
    )
```

```python
import functools

import jax
import jax.numpy as jnp
from jax import lax
from jax.experimental import pallas as pl
from jax.experimental.pallas import tpu as pltpu
from jax.sharding import PartitionSpec as P

TILE = 4
NNZ = 8
WIDTH = 128
GRID = 16
HALF = 8
SPAN = TILE * WIDTH
ROWS = NNZ * WIDTH + 16
BOTH = ("row", "col")


def even_pair(n):
    return n ^ 1


def odd_pair(n):
    return ((n - 1) ^ 1) + 1


def flat_id(i, c, role):
    layer = role ^ int((i + c) % GRID >= HALF)
    return i * 2 * GRID + c * 2 + layer


def route(step):
    pairs = []
    for i in range(GRID):
        for c in range(GRID):
            for role in range(2):
                z, y, x = step(i % HALF, c // 2, c % 2, role)
                pairs.append((flat_id(i, c, role), flat_id(i // HALF * HALF + z % HALF, (y % HALF) * 2 + x, role)))
    return pairs


def pair_of(kind, n, role):
    return even_pair(n) if kind == role else odd_pair(n)


def exchange_z(x, kind):
    return lax.ppermute(x, BOTH, route(lambda z, y, xl, r: (pair_of(kind, z, r), y, xl)))


def exchange_h(x, hop):
    def step(z, y, xl, r):
        if hop == 2:
            return z, pair_of(1, y, r), xl
        if hop == 0:
            return z, y, xl ^ 1
        return z, pair_of(0, y, r), xl

    return lax.ppermute(x, BOTH, route(step))


def pack_kernel(places_z, places_h, blocks_z, blocks_h, out_z, out_h, sem):
    lane = lax.broadcasted_iota(jnp.int32, (ROWS - NNZ * WIDTH, WIDTH), 1)
    copies = []
    for n, (blocks, out) in enumerate(((blocks_z, out_z), (blocks_h, out_h))):
        copies.append(pltpu.make_async_copy(blocks, out.at[pl.ds(0, NNZ * WIDTH)], sem.at[n]))
        copies[-1].start()
    for places, out in ((places_z, out_z), (places_h, out_h)):
        slots = jnp.zeros(lane.shape, jnp.int32)
        for k in range(NNZ):
            slots = jnp.where(lane == k, places[0, k] * TILE + places[1, k], slots)
        out[pl.ds(NNZ * WIDTH, ROWS - NNZ * WIDTH), :] = slots.astype(jnp.float32).astype(out.dtype)
    for copy in copies:
        copy.wait()


PACK_LIMIT = 56 * 1024 * 1024


def pack(places_z, places_h, blocks_z, blocks_h):
    smem = pl.BlockSpec(memory_space=pltpu.SMEM)
    hbm = pl.BlockSpec(memory_space=pl.ANY)
    vmem = pl.BlockSpec(memory_space=pltpu.VMEM)
    return pl.pallas_call(
        pack_kernel,
        out_shape=(pltpu.VMEM((ROWS, WIDTH), blocks_z.dtype),) * 2,
        in_specs=[smem, smem, hbm, hbm],
        out_specs=(vmem, vmem),
        scratch_shapes=[pltpu.SemaphoreType.DMA((2,))],
        compiler_params=pltpu.CompilerParams(vmem_limit_bytes=PACK_LIMIT),
        cost_estimate=pl.CostEstimate(flops=0, bytes_accessed=ROWS * WIDTH * 8, transcendentals=0),
        name="pack",
    )(places_z, places_h, blocks_z.reshape(NNZ * WIDTH, WIDTH), blocks_h.reshape(NNZ * WIDTH, WIDTH))


def join_kernel(a, b, out):
    out[: a.shape[0], :] = a[...]
    out[a.shape[0] :, :] = b[...]


def join(a, b, tiles=0):
    vmem = pl.BlockSpec(memory_space=pltpu.VMEM)
    rows = a.shape[0] + b.shape[0]
    return pl.pallas_call(
        join_kernel,
        out_shape=jax.ShapeDtypeStruct((rows, WIDTH), a.dtype),
        in_specs=[vmem, vmem],
        out_specs=vmem,
        compiler_params=pltpu.CompilerParams(vmem_limit_bytes=4 * 1024 * 1024),
        cost_estimate=cost(tiles, rows * WIDTH * 4),
        name="join",
    )(a, b)


def near(n, kind, role):
    even = n ^ 1
    odd = ((n - 1) ^ 1) + 1
    return jnp.where(role == kind, even, odd) & 7


def position():
    i = lax.axis_index("row")
    j = lax.axis_index("col")
    c = j >> 1
    layer = j & 1
    role = layer ^ (((i + c) & 15) >> 3)
    return i & 7, c >> 1, c & 1, layer, role


def offsets():
    z, y, xl, _, role = position()
    ya = near(y, 0, role)
    yb = near(y, 1, role)
    yab = near(yb, 0, role)
    xo = xl ^ 1
    first = ((y, xl), (y, xo), (ya, xl), (ya, xo), (yb, xl), (yb, xo), (yab, xl), (yab, xo))
    def ahead(yy, xx):
        return (2 * (yy - y) + xx - xl) & 7

    of_h = [ahead(*p) for p in first]
    up = near(z, 0, role) - z
    of_z = [(up * n) & 7 for n in (0, 1, -1, -2, 2, 3, -3, 4)]
    return of_h, of_z


def turn_of(of_h, ahead):
    turn = jnp.int32(0)
    for n in range(1, HALF):
        turn = jnp.where(of_h[n] == ahead, n, turn)
    return turn


class Slots:
    def __init__(self, parts):
        self.rows = []
        for buf, part in parts:
            base = part * ROWS + NNZ * WIDTH
            self.rows.append(buf[base : base + 16, :].astype(jnp.float32).astype(jnp.int32))

    def __getitem__(self, at):
        n, k = at
        return self.rows[n][0, k]


def place(buf, part, slots, n, put):
    for k in range(NNZ):
        row = pl.multiple_of((slots[n, k] >> 2) * WIDTH, WIDTH)
        col = pl.multiple_of((slots[n, k] & 3) * WIDTH, WIDTH)
        at = part * ROWS + k * WIDTH
        put(row, col, buf[at : at + WIDTH, :])


def into_h(dense, turn):
    def put(row, col, block):
        dense[pl.ds(row, WIDTH), pl.ds(pl.multiple_of(turn * SPAN + col, WIDTH), WIDTH)] = block

    return put


def into_z(dense, turn):
    def put(row, col, block):
        dense[pl.ds(pl.multiple_of(turn * SPAN + row, WIDTH), WIDTH), pl.ds(col, WIDTH)] = block

    return put


FIRST = 4
LAST = 2


def clear(ref):
    ref[...] = jnp.zeros_like(ref)


def keep_for_last(of_h, of_z, first_turn, parts, slots, last_h):
    for n, (buf, part) in enumerate(parts):
        for m in range(LAST):

            @pl.when(of_h[first_turn + n] == of_z[HALF - LAST + m])
            def _():
                place(buf, part, slots, n, into_h(last_h, m))


def early_kernel(hp, h1, h2, zp, z1, z2, z3, acc, mid_z, last_h, hd, zd):
    h_parts = [(hp, 0), (h1, 0), (h2, 0), (h2, 1)]
    z_parts = [(zp, 0), (z1, 0), (z2, 0), (z2, 1), (z3, 0), (z3, 1)]
    slots = Slots(h_parts + z_parts)
    for ref in (hd, zd, mid_z, last_h):
        clear(ref)
    of_h, of_z = offsets()
    for n, (buf, part) in enumerate(h_parts):
        place(buf, part, slots, n, into_h(hd, n))
    keep_for_last(of_h, of_z, 0, h_parts, slots, last_h)
    for n, (buf, part) in enumerate(z_parts):
        turn = turn_of(of_h, of_z[n])

        @pl.when(turn < FIRST)
        def _():
            place(buf, part, slots, FIRST + n, into_z(zd, turn))

        @pl.when(turn >= FIRST)
        def _():
            place(buf, part, slots, FIRST + n, into_z(mid_z, turn - FIRST))

    for m in range(0, SPAN, 256):
        acc[m : m + 256, :] = jnp.dot(hd[m : m + 256, :], zd[...], preferred_element_type=jnp.float32)


def middle_kernel(h3, h4, mid_z, acc, in_h, out_acc, last_h, hd):
    parts = [(h3, 0), (h3, 1), (h4, 0), (h4, 1)]
    slots = Slots(parts)
    clear(hd)
    of_h, of_z = offsets()
    for n, (buf, part) in enumerate(parts):
        place(buf, part, slots, n, into_h(hd, n))
    keep_for_last(of_h, of_z, FIRST, parts, slots, last_h)
    for m in range(0, SPAN, 256):
        out_acc[m : m + 256, :] = acc[m : m + 256, :] + jnp.dot(
            hd[m : m + 256, :], mid_z[...], preferred_element_type=jnp.float32
        )


def late_kernel(keep, acc, last_h, z4, own, other, zd, total):
    parts = [(z4, 0), (z4, 1)]
    slots = Slots(parts)
    clear(zd)
    layer = lax.axis_index("col") & 1
    for n, (buf, part) in enumerate(parts):
        place(buf, part, slots, n, into_z(zd, n))
    for m in range(0, SPAN, 256):
        total[m : m + 256, :] = acc[m : m + 256, :] + jnp.dot(
            last_h[m : m + 256, :], zd[...], preferred_element_type=jnp.float32
        )
    for q in range(TILE):
        for dst, first in ((own, layer * TILE), (other, (1 - layer) * TILE)):
            r = pl.multiple_of(keep[0, first + q] * WIDTH, WIDTH)
            s = pl.multiple_of(keep[1, first + q] * WIDTH, WIDTH)
            dst[q] = total[pl.ds(r, WIDTH), pl.ds(s, WIDTH)]


def finish_kernel(own, both, out):
    layer = lax.axis_index("col") & 1
    out[...] = own[...] + both[pl.ds((1 - layer) * TILE, TILE)]


VMEM = pl.BlockSpec(memory_space=pltpu.VMEM)
ACC = jax.ShapeDtypeStruct((SPAN, SPAN), jnp.float32)
LAST_H = jax.ShapeDtypeStruct((SPAN, LAST * SPAN), jnp.bfloat16)
HALF_OUT = jax.ShapeDtypeStruct((TILE, WIDTH, WIDTH), jnp.float32)


def cost(tiles, moved):
    return pl.CostEstimate(flops=2 * SPAN * SPAN * SPAN * tiles, bytes_accessed=moved, transcendentals=0)


def limit(mib):
    return pltpu.CompilerParams(vmem_limit_bytes=mib * 1024 * 1024)


def wide(tiles):
    return pltpu.VMEM((SPAN, tiles * SPAN), jnp.bfloat16)


def tall(tiles):
    return pltpu.VMEM((tiles * SPAN, SPAN), jnp.bfloat16)


def early_product(*tiles):
    return pl.pallas_call(
        early_kernel,
        out_shape=(ACC, jax.ShapeDtypeStruct((FIRST * SPAN, SPAN), jnp.bfloat16), LAST_H),
        in_specs=[VMEM] * len(tiles),
        out_specs=(VMEM,) * 3,
        scratch_shapes=[wide(FIRST), tall(FIRST)],
        compiler_params=limit(14),
        cost_estimate=cost(FIRST, 4 * 1024 * 1024),
        name="early",
    )(*tiles)


def middle_product(h3, h4, mid_z, acc, last_h):
    return pl.pallas_call(
        middle_kernel,
        out_shape=(ACC, LAST_H),
        in_specs=[VMEM] * 5,
        out_specs=(VMEM,) * 2,
        input_output_aliases={3: 0, 4: 1},
        scratch_shapes=[wide(FIRST)],
        compiler_params=limit(12),
        cost_estimate=cost(MIDDLE_TILES, 1024 * 1024),
        name="middle",
    )(h3, h4, mid_z, acc, last_h)


def late_product(keep, acc, last_h, z4):
    return pl.pallas_call(
        late_kernel,
        out_shape=(HALF_OUT, HALF_OUT),
        in_specs=[pl.BlockSpec(memory_space=pltpu.SMEM)] + [VMEM] * 3,
        out_specs=(VMEM,) * 2,
        scratch_shapes=[tall(LAST), pltpu.VMEM((SPAN, SPAN), jnp.float32)],
        compiler_params=limit(10),
        cost_estimate=cost(LAST, 2 * 1024 * 1024),
        name="late",
    )(keep, acc, last_h, z4)


def finish(own, both):
    return pl.pallas_call(
        finish_kernel,
        out_shape=HALF_OUT,
        in_specs=[VMEM] * 2,
        out_specs=VMEM,
        compiler_params=limit(4),
        cost_estimate=cost(0, 1024 * 1024),
        name="finish",
    )(own, both)


MIDDLE_TILES = 8


def per_device(h_blocks, h_index, z_blocks, z_index, keep_index):
    zp, hp = pack(z_index[0, 0], h_index[0, 0], z_blocks[0, 0], h_blocks[0, 0])
    z1 = exchange_z(zp, 0)
    h1 = exchange_h(hp, 0)
    z2 = join(exchange_z(zp, 1), exchange_z(z1, 1))
    h01 = join(hp, h1)
    h2 = exchange_h(h01, 1)
    h3 = exchange_h(h01, 2)
    z3 = exchange_z(z2, 0)
    h4 = exchange_h(h2, 2)
    z4 = exchange_z(z3, 1)
    acc, mid_z, last_h = early_product(hp, h1, h2, zp, z1, z2, z3)
    acc, last_h = middle_product(h3, h4, mid_z, acc, last_h)
    own, other = late_product(keep_index[0, 0], acc, last_h, z4)
    both = lax.all_gather(
        other, "col", axis_index_groups=[[2 * c, 2 * c + 1] for c in range(GRID)], tiled=True
    )
    return finish(own, both)[None, None]


def solution(mesh):
    return jax.shard_map(
        per_device,
        mesh=mesh,
        in_specs=(
            P("row", "col", None, None, None),
            P("row", "col", None, None),
            P("row", "col", None, None, None),
            P("row", "col", None, None),
            P("row", "col", None, None),
        ),
        out_specs=P("row", "col", None, None, None),
        check_vma=False,
    )
```

```python
import functools

import jax
import jax.numpy as jnp
from jax import lax
from jax.experimental import pallas as pl
from jax.experimental.pallas import tpu as pltpu
from jax.sharding import PartitionSpec as P

TILE = 4
NNZ = 8
WIDTH = 128
GRID = 16
HALF = 8
SPAN = TILE * WIDTH
ROWS = NNZ * WIDTH + 16
BOTH = ("row", "col")


def even_pair(n):
    return n ^ 1


def odd_pair(n):
    return ((n - 1) ^ 1) + 1


def flat_id(i, c, role):
    layer = role ^ int((i + c) % GRID >= HALF)
    return i * 2 * GRID + c * 2 + layer


def route(step):
    pairs = []
    for i in range(GRID):
        for c in range(GRID):
            for role in range(2):
                z, y, x = step(i % HALF, c // 2, c % 2, role)
                pairs.append((flat_id(i, c, role), flat_id(i // HALF * HALF + z % HALF, (y % HALF) * 2 + x, role)))
    return pairs


def pair_of(kind, n, role):
    return even_pair(n) if kind == role else odd_pair(n)


def exchange_z(x, kind):
    return lax.ppermute(x, BOTH, route(lambda z, y, xl, r: (pair_of(kind, z, r), y, xl)))


def exchange_h(x, hop):
    def step(z, y, xl, r):
        if hop == 2:
            return z, pair_of(1, y, r), xl
        if hop == 0:
            return z, y, xl ^ 1
        return z, pair_of(0, y, r), xl

    return lax.ppermute(x, BOTH, route(step))


def pack_kernel(places_z, places_h, blocks_z, blocks_h, out_z, out_h, seen, sem):
    lane = lax.broadcasted_iota(jnp.int32, (ROWS - NNZ * WIDTH, WIDTH), 1)
    copies = []
    for n, (blocks, out) in enumerate(((blocks_z, out_z), (blocks_h, out_h))):
        copies.append(pltpu.make_async_copy(blocks, out.at[pl.ds(0, NNZ * WIDTH)], sem.at[n]))
        copies[-1].start()
    lists = [pltpu.make_async_copy(p, seen.at[n], sem.at[2 + n]) for n, p in enumerate((places_z, places_h))]
    for copy in lists:
        copy.start()
    for n, out in enumerate((out_z, out_h)):
        lists[n].wait()
        slots = jnp.zeros(lane.shape, jnp.int32)
        for k in range(NNZ):
            slots = jnp.where(lane == k, seen[n, 0, k] * TILE + seen[n, 1, k], slots)
        out[pl.ds(NNZ * WIDTH, ROWS - NNZ * WIDTH), :] = slots.astype(jnp.float32).astype(out.dtype)
    for copy in copies:
        copy.wait()


PACK_LIMIT = 56 * 1024 * 1024


def pack(places_z, places_h, blocks_z, blocks_h):
    hbm = pl.BlockSpec(memory_space=pl.ANY)
    vmem = pl.BlockSpec(memory_space=pltpu.VMEM)
    return pl.pallas_call(
        pack_kernel,
        out_shape=(pltpu.VMEM((ROWS, WIDTH), blocks_z.dtype),) * 2,
        in_specs=[hbm] * 4,
        out_specs=(vmem, vmem),
        scratch_shapes=[pltpu.SMEM((2, 2, NNZ), jnp.int32), pltpu.SemaphoreType.DMA((4,))],
        compiler_params=pltpu.CompilerParams(vmem_limit_bytes=PACK_LIMIT),
        cost_estimate=pl.CostEstimate(flops=0, bytes_accessed=ROWS * WIDTH * 8, transcendentals=0),
        name="pack",
    )(places_z, places_h, blocks_z.reshape(NNZ * WIDTH, WIDTH), blocks_h.reshape(NNZ * WIDTH, WIDTH))


def join_kernel(a, b, out):
    out[: a.shape[0], :] = a[...]
    out[a.shape[0] :, :] = b[...]


def join(a, b, tiles=0):
    vmem = pl.BlockSpec(memory_space=pltpu.VMEM)
    rows = a.shape[0] + b.shape[0]
    return pl.pallas_call(
        join_kernel,
        out_shape=jax.ShapeDtypeStruct((rows, WIDTH), a.dtype),
        in_specs=[vmem, vmem],
        out_specs=vmem,
        compiler_params=pltpu.CompilerParams(vmem_limit_bytes=4 * 1024 * 1024),
        cost_estimate=cost(tiles, rows * WIDTH * 4),
        name="join",
    )(a, b)


def near(n, kind, role):
    even = n ^ 1
    odd = ((n - 1) ^ 1) + 1
    return jnp.where(role == kind, even, odd) & 7


def position():
    i = lax.axis_index("row")
    j = lax.axis_index("col")
    c = j >> 1
    layer = j & 1
    role = layer ^ (((i + c) & 15) >> 3)
    return i & 7, c >> 1, c & 1, layer, role


def offsets():
    z, y, xl, _, role = position()
    ya = near(y, 0, role)
    yb = near(y, 1, role)
    yab = near(yb, 0, role)
    xo = xl ^ 1
    first = ((y, xl), (y, xo), (ya, xl), (ya, xo), (yb, xl), (yb, xo), (yab, xl), (yab, xo))
    def ahead(yy, xx):
        return (2 * (yy - y) + xx - xl) & 7

    of_h = [ahead(*p) for p in first]
    up = near(z, 0, role) - z
    of_z = [(up * n) & 7 for n in (0, 1, -1, -2, 2, 3, -3, 4)]
    return of_h, of_z


def turn_of(of_h, ahead):
    turn = jnp.int32(0)
    for n in range(1, HALF):
        turn = jnp.where(of_h[n] == ahead, n, turn)
    return turn


class Slots:
    def __init__(self, parts):
        self.rows = []
        for buf, part in parts:
            base = part * ROWS + NNZ * WIDTH
            self.rows.append(buf[base : base + 16, :].astype(jnp.float32).astype(jnp.int32))

    def __getitem__(self, at):
        n, k = at
        return self.rows[n][0, k]


def place(buf, part, slots, n, put):
    for k in range(NNZ):
        row = pl.multiple_of((slots[n, k] >> 2) * WIDTH, WIDTH)
        col = pl.multiple_of((slots[n, k] & 3) * WIDTH, WIDTH)
        at = part * ROWS + k * WIDTH
        put(row, col, buf[at : at + WIDTH, :])


def into_h(dense, turn):
    def put(row, col, block):
        dense[pl.ds(row, WIDTH), pl.ds(pl.multiple_of(turn * SPAN + col, WIDTH), WIDTH)] = block

    return put


def into_z(dense, turn):
    def put(row, col, block):
        dense[pl.ds(pl.multiple_of(turn * SPAN + row, WIDTH), WIDTH), pl.ds(col, WIDTH)] = block

    return put


FIRST = 4
LAST = 2


def clear(ref):
    ref[...] = jnp.zeros_like(ref)


def keep_for_last(of_h, of_z, first_turn, parts, slots, last_h):
    for n, (buf, part) in enumerate(parts):
        for m in range(LAST):

            @pl.when(of_h[first_turn + n] == of_z[HALF - LAST + m])
            def _():
                place(buf, part, slots, n, into_h(last_h, m))


def early_kernel(hp, h1, h2, zp, z1, z2, z3, acc, mid_z, last_h, hd, zd):
    h_parts = [(hp, 0), (h1, 0), (h2, 0), (h2, 1)]
    z_parts = [(zp, 0), (z1, 0), (z2, 0), (z2, 1), (z3, 0), (z3, 1)]
    slots = Slots(h_parts + z_parts)
    for ref in (hd, zd, mid_z, last_h):
        clear(ref)
    of_h, of_z = offsets()
    for n, (buf, part) in enumerate(h_parts):
        place(buf, part, slots, n, into_h(hd, n))
    keep_for_last(of_h, of_z, 0, h_parts, slots, last_h)
    for n, (buf, part) in enumerate(z_parts):
        turn = turn_of(of_h, of_z[n])

        @pl.when(turn < FIRST)
        def _():
            place(buf, part, slots, FIRST + n, into_z(zd, turn))

        @pl.when(turn >= FIRST)
        def _():
            place(buf, part, slots, FIRST + n, into_z(mid_z, turn - FIRST))

    for m in range(0, SPAN, 256):
        acc[m : m + 256, :] = jnp.dot(hd[m : m + 256, :], zd[...], preferred_element_type=jnp.float32)


def middle_kernel(h3, h4, mid_z, acc, in_h, out_acc, last_h, hd):
    parts = [(h3, 0), (h3, 1), (h4, 0), (h4, 1)]
    slots = Slots(parts)
    clear(hd)
    of_h, of_z = offsets()
    for n, (buf, part) in enumerate(parts):
        place(buf, part, slots, n, into_h(hd, n))
    keep_for_last(of_h, of_z, FIRST, parts, slots, last_h)
    for m in range(0, SPAN, 256):
        out_acc[m : m + 256, :] = acc[m : m + 256, :] + jnp.dot(
            hd[m : m + 256, :], mid_z[...], preferred_element_type=jnp.float32
        )


def late_kernel(keep_list, acc, last_h, z4, own, other, zd, total, keep, sem):
    copy = pltpu.make_async_copy(keep_list, keep, sem)
    copy.start()
    parts = [(z4, 0), (z4, 1)]
    slots = Slots(parts)
    clear(zd)
    layer = lax.axis_index("col") & 1
    for n, (buf, part) in enumerate(parts):
        place(buf, part, slots, n, into_z(zd, n))
    for m in range(0, SPAN, 256):
        total[m : m + 256, :] = acc[m : m + 256, :] + jnp.dot(
            last_h[m : m + 256, :], zd[...], preferred_element_type=jnp.float32
        )
    copy.wait()
    for q in range(TILE):
        for dst, first in ((own, layer * TILE), (other, (1 - layer) * TILE)):
            r = pl.multiple_of(keep[0, first + q] * WIDTH, WIDTH)
            s = pl.multiple_of(keep[1, first + q] * WIDTH, WIDTH)
            dst[q] = total[pl.ds(r, WIDTH), pl.ds(s, WIDTH)]


def finish_kernel(own, both, out):
    layer = lax.axis_index("col") & 1
    out[...] = own[...] + both[pl.ds((1 - layer) * TILE, TILE)]


VMEM = pl.BlockSpec(memory_space=pltpu.VMEM)
ACC = jax.ShapeDtypeStruct((SPAN, SPAN), jnp.float32)
LAST_H = jax.ShapeDtypeStruct((SPAN, LAST * SPAN), jnp.bfloat16)
HALF_OUT = jax.ShapeDtypeStruct((TILE, WIDTH, WIDTH), jnp.float32)


def cost(tiles, moved):
    return pl.CostEstimate(flops=2 * SPAN * SPAN * SPAN * tiles, bytes_accessed=moved, transcendentals=0)


def limit(mib):
    return pltpu.CompilerParams(vmem_limit_bytes=mib * 1024 * 1024)


def wide(tiles):
    return pltpu.VMEM((SPAN, tiles * SPAN), jnp.bfloat16)


def tall(tiles):
    return pltpu.VMEM((tiles * SPAN, SPAN), jnp.bfloat16)


def early_product(*tiles):
    return pl.pallas_call(
        early_kernel,
        out_shape=(ACC, jax.ShapeDtypeStruct((FIRST * SPAN, SPAN), jnp.bfloat16), LAST_H),
        in_specs=[VMEM] * len(tiles),
        out_specs=(VMEM,) * 3,
        scratch_shapes=[wide(FIRST), tall(FIRST)],
        compiler_params=limit(14),
        cost_estimate=cost(FIRST, 4 * 1024 * 1024),
        name="early",
    )(*tiles)


def middle_product(h3, h4, mid_z, acc, last_h):
    return pl.pallas_call(
        middle_kernel,
        out_shape=(ACC, LAST_H),
        in_specs=[VMEM] * 5,
        out_specs=(VMEM,) * 2,
        input_output_aliases={3: 0, 4: 1},
        scratch_shapes=[wide(FIRST)],
        compiler_params=limit(12),
        cost_estimate=cost(MIDDLE_TILES, 1024 * 1024),
        name="middle",
    )(h3, h4, mid_z, acc, last_h)


def late_product(keep, acc, last_h, z4):
    return pl.pallas_call(
        late_kernel,
        out_shape=(HALF_OUT, HALF_OUT),
        in_specs=[pl.BlockSpec(memory_space=pl.ANY)] + [VMEM] * 3,
        out_specs=(VMEM,) * 2,
        scratch_shapes=[
            tall(LAST),
            pltpu.VMEM((SPAN, SPAN), jnp.float32),
            pltpu.SMEM((2, NNZ), jnp.int32),
            pltpu.SemaphoreType.DMA,
        ],
        compiler_params=limit(10),
        cost_estimate=cost(LAST, 2 * 1024 * 1024),
        name="late",
    )(keep, acc, last_h, z4)


def finish(own, both):
    return pl.pallas_call(
        finish_kernel,
        out_shape=HALF_OUT,
        in_specs=[VMEM] * 2,
        out_specs=VMEM,
        compiler_params=limit(4),
        cost_estimate=cost(0, 1024 * 1024),
        name="finish",
    )(own, both)


MIDDLE_TILES = 8


def per_device(h_blocks, h_index, z_blocks, z_index, keep_index):
    zp, hp = pack(z_index[0, 0], h_index[0, 0], z_blocks[0, 0], h_blocks[0, 0])
    z1 = exchange_z(zp, 0)
    h1 = exchange_h(hp, 0)
    z2 = join(exchange_z(zp, 1), exchange_z(z1, 1))
    h01 = join(hp, h1)
    h2 = exchange_h(h01, 1)
    h3 = exchange_h(h01, 2)
    z3 = exchange_z(z2, 0)
    h4 = exchange_h(h2, 2)
    z4 = exchange_z(z3, 1)
    acc, mid_z, last_h = early_product(hp, h1, h2, zp, z1, z2, z3)
    acc, last_h = middle_product(h3, h4, mid_z, acc, last_h)
    own, other = late_product(keep_index[0, 0], acc, last_h, z4)
    both = lax.all_gather(
        other, "col", axis_index_groups=[[2 * c, 2 * c + 1] for c in range(GRID)], tiled=True
    )
    return finish(own, both)[None, None]


def solution(mesh):
    return jax.shard_map(
        per_device,
        mesh=mesh,
        in_specs=(
            P("row", "col", None, None, None),
            P("row", "col", None, None),
            P("row", "col", None, None, None),
            P("row", "col", None, None),
            P("row", "col", None, None),
        ),
        out_specs=P("row", "col", None, None, None),
        check_vma=False,
    )
```

```python
import functools

import jax
import jax.numpy as jnp
from jax import lax
from jax.experimental import pallas as pl
from jax.experimental.pallas import tpu as pltpu
from jax.sharding import PartitionSpec as P

TILE = 4
NNZ = 8
WIDTH = 128
GRID = 16
HALF = 8
SPAN = TILE * WIDTH
ROWS = NNZ * WIDTH + 16
BOTH = ("row", "col")


def even_pair(n):
    return n ^ 1


def odd_pair(n):
    return ((n - 1) ^ 1) + 1


def flat_id(i, c, role):
    layer = role ^ int((i + c) % GRID >= HALF)
    return i * 2 * GRID + c * 2 + layer


def route(step):
    pairs = []
    for i in range(GRID):
        for c in range(GRID):
            for role in range(2):
                z, y, x = step(i % HALF, c // 2, c % 2, role)
                pairs.append((flat_id(i, c, role), flat_id(i // HALF * HALF + z % HALF, (y % HALF) * 2 + x, role)))
    return pairs


def pair_of(kind, n, role):
    return even_pair(n) if kind == role else odd_pair(n)


def exchange_z(x, kind):
    return lax.ppermute(x, BOTH, route(lambda z, y, xl, r: (pair_of(1 - kind, z, r), y, xl)))


def exchange_h(x, hop):
    def step(z, y, xl, r):
        if hop == 2:
            return z, pair_of(1, y, r), xl
        if hop == 0:
            return z, y, xl ^ 1
        return z, pair_of(0, y, r), xl

    return lax.ppermute(x, BOTH, route(step))


def pack_kernel(places_z, places_h, blocks_z, blocks_h, out_z, out_h, seen, sem):
    lane = lax.broadcasted_iota(jnp.int32, (ROWS - NNZ * WIDTH, WIDTH), 1)
    copies = []
    for n, (blocks, out) in enumerate(((blocks_z, out_z), (blocks_h, out_h))):
        copies.append(pltpu.make_async_copy(blocks, out.at[pl.ds(0, NNZ * WIDTH)], sem.at[n]))
        copies[-1].start()
    lists = [pltpu.make_async_copy(p, seen.at[n], sem.at[2 + n]) for n, p in enumerate((places_z, places_h))]
    for copy in lists:
        copy.start()
    for n, out in enumerate((out_z, out_h)):
        lists[n].wait()
        slots = jnp.zeros(lane.shape, jnp.int32)
        for k in range(NNZ):
            slots = jnp.where(lane == k, seen[n, 0, k] * TILE + seen[n, 1, k], slots)
        out[pl.ds(NNZ * WIDTH, ROWS - NNZ * WIDTH), :] = slots.astype(jnp.float32).astype(out.dtype)
    for copy in copies:
        copy.wait()


PACK_LIMIT = 56 * 1024 * 1024


def pack(places_z, places_h, blocks_z, blocks_h):
    hbm = pl.BlockSpec(memory_space=pl.ANY)
    vmem = pl.BlockSpec(memory_space=pltpu.VMEM)
    return pl.pallas_call(
        pack_kernel,
        out_shape=(pltpu.VMEM((ROWS, WIDTH), blocks_z.dtype),) * 2,
        in_specs=[hbm] * 4,
        out_specs=(vmem, vmem),
        scratch_shapes=[pltpu.SMEM((2, 2, NNZ), jnp.int32), pltpu.SemaphoreType.DMA((4,))],
        compiler_params=pltpu.CompilerParams(vmem_limit_bytes=PACK_LIMIT),
        cost_estimate=pl.CostEstimate(flops=0, bytes_accessed=ROWS * WIDTH * 8, transcendentals=0),
        name="pack",
    )(places_z, places_h, blocks_z.reshape(NNZ * WIDTH, WIDTH), blocks_h.reshape(NNZ * WIDTH, WIDTH))


def join_kernel(a, b, out):
    out[: a.shape[0], :] = a[...]
    out[a.shape[0] :, :] = b[...]


def join(a, b, tiles=0):
    vmem = pl.BlockSpec(memory_space=pltpu.VMEM)
    rows = a.shape[0] + b.shape[0]
    return pl.pallas_call(
        join_kernel,
        out_shape=jax.ShapeDtypeStruct((rows, WIDTH), a.dtype),
        in_specs=[vmem, vmem],
        out_specs=vmem,
        compiler_params=pltpu.CompilerParams(vmem_limit_bytes=4 * 1024 * 1024),
        cost_estimate=cost(tiles, rows * WIDTH * 4),
        name="join",
    )(a, b)


def near(n, kind, role):
    even = n ^ 1
    odd = ((n - 1) ^ 1) + 1
    return jnp.where(role == kind, even, odd) & 7


def position():
    i = lax.axis_index("row")
    j = lax.axis_index("col")
    c = j >> 1
    layer = j & 1
    role = layer ^ (((i + c) & 15) >> 3)
    return i & 7, c >> 1, c & 1, layer, role


def offsets():
    z, y, xl, _, role = position()
    ya = near(y, 0, role)
    yb = near(y, 1, role)
    yab = near(yb, 0, role)
    xo = xl ^ 1
    first = ((y, xl), (y, xo), (ya, xl), (ya, xo), (yb, xl), (yb, xo), (yab, xl), (yab, xo))
    def ahead(yy, xx):
        return (2 * (yy - y) + xx - xl) & 7

    of_h = [ahead(*p) for p in first]
    up = near(z, 1, role) - z
    of_z = [(up * n) & 7 for n in (0, 1, -1, -2, 2, 3, -3, 4)]
    return of_h, of_z


def turn_of(of_h, ahead):
    turn = jnp.int32(0)
    for n in range(1, HALF):
        turn = jnp.where(of_h[n] == ahead, n, turn)
    return turn


class Slots:
    def __init__(self, parts):
        self.rows = []
        for buf, part in parts:
            base = part * ROWS + NNZ * WIDTH
            self.rows.append(buf[base : base + 16, :].astype(jnp.float32).astype(jnp.int32))

    def __getitem__(self, at):
        n, k = at
        return self.rows[n][0, k]


def place(buf, part, slots, n, put):
    for k in range(NNZ):
        row = pl.multiple_of((slots[n, k] >> 2) * WIDTH, WIDTH)
        col = pl.multiple_of((slots[n, k] & 3) * WIDTH, WIDTH)
        at = part * ROWS + k * WIDTH
        put(row, col, buf[at : at + WIDTH, :])


def into_h(dense, turn):
    def put(row, col, block):
        dense[pl.ds(row, WIDTH), pl.ds(pl.multiple_of(turn * SPAN + col, WIDTH), WIDTH)] = block

    return put


def into_z(dense, turn):
    def put(row, col, block):
        dense[pl.ds(pl.multiple_of(turn * SPAN + row, WIDTH), WIDTH), pl.ds(col, WIDTH)] = block

    return put


FIRST = 4
LAST = 2


def clear(ref):
    ref[...] = jnp.zeros_like(ref)


def keep_for_last(of_h, of_z, first_turn, parts, slots, last_h):
    for n, (buf, part) in enumerate(parts):
        for m in range(LAST):

            @pl.when(of_h[first_turn + n] == of_z[HALF - LAST + m])
            def _():
                place(buf, part, slots, n, into_h(last_h, m))


def early_kernel(hp, h1, h2, zp, z1, z2, z3, acc, mid_z, last_h, hd, zd):
    h_parts = [(hp, 0), (h1, 0), (h2, 0), (h2, 1)]
    z_parts = [(zp, 0), (z1, 0), (z2, 0), (z2, 1), (z3, 0), (z3, 1)]
    slots = Slots(h_parts + z_parts)
    for ref in (hd, zd, mid_z, last_h):
        clear(ref)
    of_h, of_z = offsets()
    for n, (buf, part) in enumerate(h_parts):
        place(buf, part, slots, n, into_h(hd, n))
    keep_for_last(of_h, of_z, 0, h_parts, slots, last_h)
    for n, (buf, part) in enumerate(z_parts):
        turn = turn_of(of_h, of_z[n])

        @pl.when(turn < FIRST)
        def _():
            place(buf, part, slots, FIRST + n, into_z(zd, turn))

        @pl.when(turn >= FIRST)
        def _():
            place(buf, part, slots, FIRST + n, into_z(mid_z, turn - FIRST))

    for m in range(0, SPAN, 256):
        acc[m : m + 256, :] = jnp.dot(hd[m : m + 256, :], zd[...], preferred_element_type=jnp.float32)


def middle_kernel(h3, h4, mid_z, acc, in_h, out_acc, last_h, hd):
    parts = [(h3, 0), (h3, 1), (h4, 0), (h4, 1)]
    slots = Slots(parts)
    clear(hd)
    of_h, of_z = offsets()
    for n, (buf, part) in enumerate(parts):
        place(buf, part, slots, n, into_h(hd, n))
    keep_for_last(of_h, of_z, FIRST, parts, slots, last_h)
    for m in range(0, SPAN, 256):
        out_acc[m : m + 256, :] = acc[m : m + 256, :] + jnp.dot(
            hd[m : m + 256, :], mid_z[...], preferred_element_type=jnp.float32
        )


def late_kernel(keep_list, acc, last_h, z4, own, other, zd, total, keep, sem):
    copy = pltpu.make_async_copy(keep_list, keep, sem)
    copy.start()
    parts = [(z4, 0), (z4, 1)]
    slots = Slots(parts)
    clear(zd)
    layer = lax.axis_index("col") & 1
    for n, (buf, part) in enumerate(parts):
        place(buf, part, slots, n, into_z(zd, n))
    for m in range(0, SPAN, 256):
        total[m : m + 256, :] = acc[m : m + 256, :] + jnp.dot(
            last_h[m : m + 256, :], zd[...], preferred_element_type=jnp.float32
        )
    copy.wait()
    for q in range(TILE):
        for dst, first in ((own, layer * TILE), (other, (1 - layer) * TILE)):
            r = pl.multiple_of(keep[0, first + q] * WIDTH, WIDTH)
            s = pl.multiple_of(keep[1, first + q] * WIDTH, WIDTH)
            dst[q] = total[pl.ds(r, WIDTH), pl.ds(s, WIDTH)]


def finish_kernel(own, both, out):
    layer = lax.axis_index("col") & 1
    out[...] = own[...] + both[pl.ds((1 - layer) * TILE, TILE)]


VMEM = pl.BlockSpec(memory_space=pltpu.VMEM)
ACC = jax.ShapeDtypeStruct((SPAN, SPAN), jnp.float32)
LAST_H = jax.ShapeDtypeStruct((SPAN, LAST * SPAN), jnp.bfloat16)
HALF_OUT = jax.ShapeDtypeStruct((TILE, WIDTH, WIDTH), jnp.float32)


def cost(tiles, moved):
    return pl.CostEstimate(flops=2 * SPAN * SPAN * SPAN * tiles, bytes_accessed=moved, transcendentals=0)


def limit(mib):
    return pltpu.CompilerParams(vmem_limit_bytes=mib * 1024 * 1024)


def wide(tiles):
    return pltpu.VMEM((SPAN, tiles * SPAN), jnp.bfloat16)


def tall(tiles):
    return pltpu.VMEM((tiles * SPAN, SPAN), jnp.bfloat16)


def early_product(*tiles):
    return pl.pallas_call(
        early_kernel,
        out_shape=(ACC, jax.ShapeDtypeStruct((FIRST * SPAN, SPAN), jnp.bfloat16), LAST_H),
        in_specs=[VMEM] * len(tiles),
        out_specs=(VMEM,) * 3,
        scratch_shapes=[wide(FIRST), tall(FIRST)],
        compiler_params=limit(14),
        cost_estimate=cost(FIRST, 4 * 1024 * 1024),
        name="early",
    )(*tiles)


def middle_product(h3, h4, mid_z, acc, last_h):
    return pl.pallas_call(
        middle_kernel,
        out_shape=(ACC, LAST_H),
        in_specs=[VMEM] * 5,
        out_specs=(VMEM,) * 2,
        input_output_aliases={3: 0, 4: 1},
        scratch_shapes=[wide(FIRST)],
        compiler_params=limit(12),
        cost_estimate=cost(MIDDLE_TILES, 1024 * 1024),
        name="middle",
    )(h3, h4, mid_z, acc, last_h)


def late_product(keep, acc, last_h, z4):
    return pl.pallas_call(
        late_kernel,
        out_shape=(HALF_OUT, HALF_OUT),
        in_specs=[pl.BlockSpec(memory_space=pl.ANY)] + [VMEM] * 3,
        out_specs=(VMEM,) * 2,
        scratch_shapes=[
            tall(LAST),
            pltpu.VMEM((SPAN, SPAN), jnp.float32),
            pltpu.SMEM((2, NNZ), jnp.int32),
            pltpu.SemaphoreType.DMA,
        ],
        compiler_params=limit(10),
        cost_estimate=cost(LAST, 2 * 1024 * 1024),
        name="late",
    )(keep, acc, last_h, z4)


def finish(own, both):
    return pl.pallas_call(
        finish_kernel,
        out_shape=HALF_OUT,
        in_specs=[VMEM] * 2,
        out_specs=VMEM,
        compiler_params=limit(4),
        cost_estimate=cost(0, 1024 * 1024),
        name="finish",
    )(own, both)


MIDDLE_TILES = 8


def per_device(h_blocks, h_index, z_blocks, z_index, keep_index):
    zp, hp = pack(z_index[0, 0], h_index[0, 0], z_blocks[0, 0], h_blocks[0, 0])
    z1 = exchange_z(zp, 0)
    h1 = exchange_h(hp, 0)
    z2 = join(exchange_z(zp, 1), exchange_z(z1, 1))
    h01 = join(hp, h1)
    h2 = exchange_h(h01, 1)
    h3 = exchange_h(h01, 2)
    z3 = exchange_z(z2, 0)
    h4 = exchange_h(h2, 2)
    z4 = exchange_z(z3, 1)
    acc, mid_z, last_h = early_product(hp, h1, h2, zp, z1, z2, z3)
    acc, last_h = middle_product(h3, h4, mid_z, acc, last_h)
    own, other = late_product(keep_index[0, 0], acc, last_h, z4)
    both = lax.all_gather(
        other, "col", axis_index_groups=[[2 * c, 2 * c + 1] for c in range(GRID)], tiled=True
    )
    return finish(own, both)[None, None]


def solution(mesh):
    return jax.shard_map(
        per_device,
        mesh=mesh,
        in_specs=(
            P("row", "col", None, None, None),
            P("row", "col", None, None),
            P("row", "col", None, None, None),
            P("row", "col", None, None),
            P("row", "col", None, None),
        ),
        out_specs=P("row", "col", None, None, None),
        check_vma=False,
    )
```

```python
import functools

import jax
import jax.numpy as jnp
from jax import lax
from jax.experimental import pallas as pl
from jax.experimental.pallas import tpu as pltpu
from jax.sharding import PartitionSpec as P

TILE = 4
NNZ = 8
WIDTH = 128
GRID = 16
HALF = 8
SPAN = TILE * WIDTH
ROWS = NNZ * WIDTH + 16
BOTH = ("row", "col")


def even_pair(n):
    return n ^ 1


def odd_pair(n):
    return ((n - 1) ^ 1) + 1


def flat_id(i, c, role):
    layer = role ^ int((i + c) % GRID >= HALF)
    return i * 2 * GRID + c * 2 + layer


def route(step):
    pairs = []
    for i in range(GRID):
        for c in range(GRID):
            for role in range(2):
                z, y, x = step(i % HALF, c // 2, c % 2, role)
                pairs.append((flat_id(i, c, role), flat_id(i // HALF * HALF + z % HALF, (y % HALF) * 2 + x, role)))
    return pairs


def pair_of(kind, n, role):
    return even_pair(n) if kind == role else odd_pair(n)


def exchange_z(x, kind):
    return lax.ppermute(x, BOTH, route(lambda z, y, xl, r: (pair_of(1 - kind, z, r), y, xl)))


def exchange_h(x, hop):
    def step(z, y, xl, r):
        if hop == 2:
            return z, pair_of(0, y, r), xl
        if hop == 0:
            return z, y, xl ^ 1
        return z, pair_of(1, y, r), xl

    return lax.ppermute(x, BOTH, route(step))


def pack_kernel(places_z, places_h, blocks_z, blocks_h, out_z, out_h, seen, sem):
    lane = lax.broadcasted_iota(jnp.int32, (ROWS - NNZ * WIDTH, WIDTH), 1)
    copies = []
    for n, (blocks, out) in enumerate(((blocks_z, out_z), (blocks_h, out_h))):
        copies.append(pltpu.make_async_copy(blocks, out.at[pl.ds(0, NNZ * WIDTH)], sem.at[n]))
        copies[-1].start()
    lists = [pltpu.make_async_copy(p, seen.at[n], sem.at[2 + n]) for n, p in enumerate((places_z, places_h))]
    for copy in lists:
        copy.start()
    for n, out in enumerate((out_z, out_h)):
        lists[n].wait()
        slots = jnp.zeros(lane.shape, jnp.int32)
        for k in range(NNZ):
            slots = jnp.where(lane == k, seen[n, 0, k] * TILE + seen[n, 1, k], slots)
        out[pl.ds(NNZ * WIDTH, ROWS - NNZ * WIDTH), :] = slots.astype(jnp.float32).astype(out.dtype)
    for copy in copies:
        copy.wait()


PACK_LIMIT = 56 * 1024 * 1024


def pack(places_z, places_h, blocks_z, blocks_h):
    hbm = pl.BlockSpec(memory_space=pl.ANY)
    vmem = pl.BlockSpec(memory_space=pltpu.VMEM)
    return pl.pallas_call(
        pack_kernel,
        out_shape=(pltpu.VMEM((ROWS, WIDTH), blocks_z.dtype),) * 2,
        in_specs=[hbm] * 4,
        out_specs=(vmem, vmem),
        scratch_shapes=[pltpu.SMEM((2, 2, NNZ), jnp.int32), pltpu.SemaphoreType.DMA((4,))],
        compiler_params=pltpu.CompilerParams(vmem_limit_bytes=PACK_LIMIT),
        cost_estimate=pl.CostEstimate(flops=0, bytes_accessed=ROWS * WIDTH * 8, transcendentals=0),
        name="pack",
    )(places_z, places_h, blocks_z.reshape(NNZ * WIDTH, WIDTH), blocks_h.reshape(NNZ * WIDTH, WIDTH))


def join_kernel(a, b, out):
    out[: a.shape[0], :] = a[...]
    out[a.shape[0] :, :] = b[...]


def join(a, b, tiles=0):
    vmem = pl.BlockSpec(memory_space=pltpu.VMEM)
    rows = a.shape[0] + b.shape[0]
    return pl.pallas_call(
        join_kernel,
        out_shape=jax.ShapeDtypeStruct((rows, WIDTH), a.dtype),
        in_specs=[vmem, vmem],
        out_specs=vmem,
        compiler_params=pltpu.CompilerParams(vmem_limit_bytes=4 * 1024 * 1024),
        cost_estimate=cost(tiles, rows * WIDTH * 4),
        name="join",
    )(a, b)


def near(n, kind, role):
    even = n ^ 1
    odd = ((n - 1) ^ 1) + 1
    return jnp.where(role == kind, even, odd) & 7


def position():
    i = lax.axis_index("row")
    j = lax.axis_index("col")
    c = j >> 1
    layer = j & 1
    role = layer ^ (((i + c) & 15) >> 3)
    return i & 7, c >> 1, c & 1, layer, role


def offsets():
    z, y, xl, _, role = position()
    ya = near(y, 1, role)
    yb = near(y, 0, role)
    yab = near(yb, 1, role)
    xo = xl ^ 1
    first = ((y, xl), (y, xo), (ya, xl), (ya, xo), (yb, xl), (yb, xo), (yab, xl), (yab, xo))
    def ahead(yy, xx):
        return (2 * (yy - y) + xx - xl) & 7

    of_h = [ahead(*p) for p in first]
    up = near(z, 1, role) - z
    of_z = [(up * n) & 7 for n in (0, 1, -1, -2, 2, 3, -3, 4)]
    return of_h, of_z


def turn_of(of_h, ahead):
    turn = jnp.int32(0)
    for n in range(1, HALF):
        turn = jnp.where(of_h[n] == ahead, n, turn)
    return turn


class Slots:
    def __init__(self, parts):
        self.rows = []
        for buf, part in parts:
            base = part * ROWS + NNZ * WIDTH
            self.rows.append(buf[base : base + 16, :].astype(jnp.float32).astype(jnp.int32))

    def __getitem__(self, at):
        n, k = at
        return self.rows[n][0, k]


def place(buf, part, slots, n, put):
    for k in range(NNZ):
        row = pl.multiple_of((slots[n, k] >> 2) * WIDTH, WIDTH)
        col = pl.multiple_of((slots[n, k] & 3) * WIDTH, WIDTH)
        at = part * ROWS + k * WIDTH
        put(row, col, buf[at : at + WIDTH, :])


def into_h(dense, turn):
    def put(row, col, block):
        dense[pl.ds(row, WIDTH), pl.ds(pl.multiple_of(turn * SPAN + col, WIDTH), WIDTH)] = block

    return put


def into_z(dense, turn):
    def put(row, col, block):
        dense[pl.ds(pl.multiple_of(turn * SPAN + row, WIDTH), WIDTH), pl.ds(col, WIDTH)] = block

    return put


FIRST = 4
LAST = 2


def clear(ref):
    ref[...] = jnp.zeros_like(ref)


def keep_for_last(of_h, of_z, first_turn, parts, slots, last_h):
    for n, (buf, part) in enumerate(parts):
        for m in range(LAST):

            @pl.when(of_h[first_turn + n] == of_z[HALF - LAST + m])
            def _():
                place(buf, part, slots, n, into_h(last_h, m))


def early_kernel(hp, h1, h2, zp, z1, z2, z3, acc, mid_z, last_h, hd, zd):
    h_parts = [(hp, 0), (h1, 0), (h2, 0), (h2, 1)]
    z_parts = [(zp, 0), (z1, 0), (z2, 0), (z2, 1), (z3, 0), (z3, 1)]
    slots = Slots(h_parts + z_parts)
    for ref in (hd, zd, mid_z, last_h):
        clear(ref)
    of_h, of_z = offsets()
    for n, (buf, part) in enumerate(h_parts):
        place(buf, part, slots, n, into_h(hd, n))
    keep_for_last(of_h, of_z, 0, h_parts, slots, last_h)
    for n, (buf, part) in enumerate(z_parts):
        turn = turn_of(of_h, of_z[n])

        @pl.when(turn < FIRST)
        def _():
            place(buf, part, slots, FIRST + n, into_z(zd, turn))

        @pl.when(turn >= FIRST)
        def _():
            place(buf, part, slots, FIRST + n, into_z(mid_z, turn - FIRST))

    for m in range(0, SPAN, 256):
        acc[m : m + 256, :] = jnp.dot(hd[m : m + 256, :], zd[...], preferred_element_type=jnp.float32)


def middle_kernel(h3, h4, mid_z, acc, in_h, out_acc, last_h, hd):
    parts = [(h3, 0), (h3, 1), (h4, 0), (h4, 1)]
    slots = Slots(parts)
    clear(hd)
    of_h, of_z = offsets()
    for n, (buf, part) in enumerate(parts):
        place(buf, part, slots, n, into_h(hd, n))
    keep_for_last(of_h, of_z, FIRST, parts, slots, last_h)
    for m in range(0, SPAN, 256):
        out_acc[m : m + 256, :] = acc[m : m + 256, :] + jnp.dot(
            hd[m : m + 256, :], mid_z[...], preferred_element_type=jnp.float32
        )


def late_kernel(keep_list, acc, last_h, z4, own, other, zd, total, keep, sem):
    copy = pltpu.make_async_copy(keep_list, keep, sem)
    copy.start()
    parts = [(z4, 0), (z4, 1)]
    slots = Slots(parts)
    clear(zd)
    layer = lax.axis_index("col") & 1
    for n, (buf, part) in enumerate(parts):
        place(buf, part, slots, n, into_z(zd, n))
    for m in range(0, SPAN, 256):
        total[m : m + 256, :] = acc[m : m + 256, :] + jnp.dot(
            last_h[m : m + 256, :], zd[...], preferred_element_type=jnp.float32
        )
    copy.wait()
    for q in range(TILE):
        for dst, first in ((own, layer * TILE), (other, (1 - layer) * TILE)):
            r = pl.multiple_of(keep[0, first + q] * WIDTH, WIDTH)
            s = pl.multiple_of(keep[1, first + q] * WIDTH, WIDTH)
            dst[q] = total[pl.ds(r, WIDTH), pl.ds(s, WIDTH)]


def finish_kernel(own, both, out):
    layer = lax.axis_index("col") & 1
    out[...] = own[...] + both[pl.ds((1 - layer) * TILE, TILE)]


VMEM = pl.BlockSpec(memory_space=pltpu.VMEM)
ACC = jax.ShapeDtypeStruct((SPAN, SPAN), jnp.float32)
LAST_H = jax.ShapeDtypeStruct((SPAN, LAST * SPAN), jnp.bfloat16)
HALF_OUT = jax.ShapeDtypeStruct((TILE, WIDTH, WIDTH), jnp.float32)


def cost(tiles, moved):
    return pl.CostEstimate(flops=2 * SPAN * SPAN * SPAN * tiles, bytes_accessed=moved, transcendentals=0)


def limit(mib):
    return pltpu.CompilerParams(vmem_limit_bytes=mib * 1024 * 1024)


def wide(tiles):
    return pltpu.VMEM((SPAN, tiles * SPAN), jnp.bfloat16)


def tall(tiles):
    return pltpu.VMEM((tiles * SPAN, SPAN), jnp.bfloat16)


def early_product(*tiles):
    return pl.pallas_call(
        early_kernel,
        out_shape=(ACC, jax.ShapeDtypeStruct((FIRST * SPAN, SPAN), jnp.bfloat16), LAST_H),
        in_specs=[VMEM] * len(tiles),
        out_specs=(VMEM,) * 3,
        scratch_shapes=[wide(FIRST), tall(FIRST)],
        compiler_params=limit(14),
        cost_estimate=cost(FIRST, 4 * 1024 * 1024),
        name="early",
    )(*tiles)


def middle_product(h3, h4, mid_z, acc, last_h):
    return pl.pallas_call(
        middle_kernel,
        out_shape=(ACC, LAST_H),
        in_specs=[VMEM] * 5,
        out_specs=(VMEM,) * 2,
        input_output_aliases={3: 0, 4: 1},
        scratch_shapes=[wide(FIRST)],
        compiler_params=limit(12),
        cost_estimate=cost(MIDDLE_TILES, 1024 * 1024),
        name="middle",
    )(h3, h4, mid_z, acc, last_h)


def late_product(keep, acc, last_h, z4):
    return pl.pallas_call(
        late_kernel,
        out_shape=(HALF_OUT, HALF_OUT),
        in_specs=[pl.BlockSpec(memory_space=pl.ANY)] + [VMEM] * 3,
        out_specs=(VMEM,) * 2,
        scratch_shapes=[
            tall(LAST),
            pltpu.VMEM((SPAN, SPAN), jnp.float32),
            pltpu.SMEM((2, NNZ), jnp.int32),
            pltpu.SemaphoreType.DMA,
        ],
        compiler_params=limit(10),
        cost_estimate=cost(LAST, 2 * 1024 * 1024),
        name="late",
    )(keep, acc, last_h, z4)


def finish(own, both):
    return pl.pallas_call(
        finish_kernel,
        out_shape=HALF_OUT,
        in_specs=[VMEM] * 2,
        out_specs=VMEM,
        compiler_params=limit(4),
        cost_estimate=cost(0, 1024 * 1024),
        name="finish",
    )(own, both)


MIDDLE_TILES = 8


def per_device(h_blocks, h_index, z_blocks, z_index, keep_index):
    zp, hp = pack(z_index[0, 0], h_index[0, 0], z_blocks[0, 0], h_blocks[0, 0])
    z1 = exchange_z(zp, 0)
    h1 = exchange_h(hp, 0)
    z2 = join(exchange_z(zp, 1), exchange_z(z1, 1))
    h01 = join(hp, h1)
    h2 = exchange_h(h01, 1)
    h3 = exchange_h(h01, 2)
    z3 = exchange_z(z2, 0)
    h4 = exchange_h(h2, 2)
    z4 = exchange_z(z3, 1)
    acc, mid_z, last_h = early_product(hp, h1, h2, zp, z1, z2, z3)
    acc, last_h = middle_product(h3, h4, mid_z, acc, last_h)
    own, other = late_product(keep_index[0, 0], acc, last_h, z4)
    both = lax.all_gather(
        other, "col", axis_index_groups=[[2 * c, 2 * c + 1] for c in range(GRID)], tiled=True
    )
    return finish(own, both)[None, None]


def solution(mesh):
    return jax.shard_map(
        per_device,
        mesh=mesh,
        in_specs=(
            P("row", "col", None, None, None),
            P("row", "col", None, None),
            P("row", "col", None, None, None),
            P("row", "col", None, None),
            P("row", "col", None, None),
        ),
        out_specs=P("row", "col", None, None, None),
        check_vma=False,
    )
```
